32 devices in a mesh: dp: 8 (over z, x), tensor: 4 (over y, core).
Axes of the slice: x: 2, y: 2, z: 4, core: 2. Of those that a mesh axis runs over, the one named last changes fastest.
Arguments:
- hidden_in: bfloat16 [8, 512, 2048], P('dp', 'tensor'), may hold values from -6 to 6
- out_grad: bfloat16 [8, 512, 2048], P('dp', 'tensor'), may hold values from -6 to 6
- doc_lengths: int32 [8, 4], P('dp'), may hold values from 1 to 384, 512 in all within a row
- norm_gains: float32 [2, 2048], replicated, may hold values from 0.5 to 1.5
- w_query: float32 [2048, 2048], P('dp', 'tensor'), may hold values from -0.125 to 0.125
- w_keyval: float32 [2, 2048, 512], P(None, 'dp', 'tensor'), may hold values from -0.125 to 0.125
- w_out: float32 [2048, 2048], P('tensor', 'dp'), may hold values from -1 to 1
- w_gateup: float32 [2, 2048, 8192], P(None, 'dp', 'tensor'), may hold values from -0.125 to 0.125
- w_down: float32 [8192, 2048], P('tensor', 'dp'), may hold values from -0.0625 to 0.0625
- moment_gains: float32 [2, 2048], replicated, may hold values from -448 to 448
- moment_query: float32 [2048, 2048], P('dp', 'tensor'), may hold values from -192 to 192
- moment_keyval: float32 [2, 2048, 512], P(None, 'dp', 'tensor'), may hold values from -256 to 256
- moment_out: float32 [2048, 2048], P('tensor', 'dp'), may hold values from -56 to 56
- moment_gateup: float32 [2, 2048, 8192], P(None, 'dp', 'tensor'), may hold values from -192 to 192
- moment_down: float32 [8192, 2048], P('tensor', 'dp'), may hold values from -224 to 224
- second_gains: float32 [2, 2048], replicated, may hold values from 5898.24 to 23592.96
- second_query: float32 [2048, 2048], P('dp', 'tensor'), may hold values from 1024 to 4096
- second_keyval: float32 [2, 2048, 512], P(None, 'dp', 'tensor'), may hold values from 2007.04 to 8028.16
- second_out: float32 [2048, 2048], P('tensor', 'dp'), may hold values from 92.16 to 368.64
- second_gateup: float32 [2, 2048, 8192], P(None, 'dp', 'tensor'), may hold values from 1024 to 4096
- second_down: float32 [8192, 2048], P('tensor', 'dp'), may hold values from 1474.56 to 5898.24
Outputs:
- block_out: bfloat16 [8, 512, 2048], P('dp', 'tensor')
- input_grad: float32 [8, 512, 2048], P('dp', 'tensor')
- grad_gains: float32 [2, 2048], replicated
- grad_query: float32 [2048, 2048], P('dp', 'tensor')
- grad_keyval: float32 [2, 2048, 512], P(None, 'dp', 'tensor')
- grad_out: float32 [2048, 2048], P('tensor', 'dp')
- grad_gateup: float32 [2, 2048, 8192], P(None, 'dp', 'tensor')
- grad_down: float32 [8192, 2048], P('tensor', 'dp')
- new_gains: float32 [2, 2048], replicated
- new_query: float32 [2048, 2048], P('dp', 'tensor')
- new_keyval: float32 [2, 2048, 512], P(None, 'dp', 'tensor')
- new_out: float32 [2048, 2048], P('tensor', 'dp')
- new_gateup: float32 [2, 2048, 8192], P(None, 'dp', 'tensor')
- new_down: float32 [8192, 2048], P('tensor', 'dp')
- new_moment_gains: float32 [2, 2048], replicated
- new_moment_query: float32 [2048, 2048], P('dp', 'tensor')
- new_moment_keyval: float32 [2, 2048, 512], P(None, 'dp', 'tensor')
- new_moment_out: float32 [2048, 2048], P('tensor', 'dp')
- new_moment_gateup: float32 [2, 2048, 8192], P(None, 'dp', 'tensor')
- new_moment_down: float32 [8192, 2048], P('tensor', 'dp')
- new_second_gains: float32 [2, 2048], replicated
- new_second_query: float32 [2048, 2048], P('dp', 'tensor')
- new_second_keyval: float32 [2, 2048, 512], P(None, 'dp', 'tensor')
- new_second_out: float32 [2048, 2048], P('tensor', 'dp')
- new_second_gateup: float32 [2, 2048, 8192], P(None, 'dp', 'tensor')
- new_second_down: float32 [8192, 2048], P('tensor', 'dp')
- weight_norms: float32 [9], replicated
- update_norms: float32 [9], replicated
- trust_ratios: float32 [9], replicated
The draws below stay inside these ranges and needn't reach their ends.
Inputs may be any that keep to these rules, and one draw needn't show every extreme that they name: `doc_lengths`: each row's 4 lengths add up to 512, and the longest is exactly 384.
All inputs are finite; a program needn't handle non-finite values.
Results may differ from the reference program's by a relative error of at most 0.015.
Values may be sent and summed in bfloat16 or wider, within the bound.
No kernel may reach another device: no remote copies, remote signals or barrier semaphores. Data moves between devices by JAX's collectives and lax.ppermute only.
A program may use at most 256 MiB of HBM per device.

```python
import math
import jax
import jax.numpy as jnp
import numpy as np
from jax import lax

D = 2048
H = 32
KV = 8
HD = 64
FF = 8192
NDOC = 4
ROW_LEN = 512
ROWS = 8
TOKENS = 4096
DOC_MOST = 384


def level_of(rng, shape, split, least, largest):
    gain, own = 1.0, jax.random.fold_in(rng, 6)
    for axis_at, shards_of in split:
        steps = jnp.exp(jax.random.uniform(jax.random.fold_in(own, axis_at), (shards_of,), jnp.float32, least / len(split), largest / len(split)))
        gain = gain * jnp.repeat(steps, shape[axis_at] // shards_of).reshape([-1 if axis == axis_at else 1 for axis in range(len(shape))])
    return gain


def length_profile(amount, total, most, skew):
    loads = [(1 << 20) // math.isqrt(rank ** skew) + 1 for rank in range(2, amount + 1)]
    spare, counts = total - most - (amount - 1), [1] * (amount - 1)
    while spare > 0:
        free = [i for i in range(amount - 1) if counts[i] < most]
        pool, remaining = sum([loads[i] for i in free]), spare
        for i in free:
            more = min(most - counts[i], max(1, remaining * loads[i] // pool), spare)
            counts[i] = counts[i] + more
            spare = spare - more
    return np.array([most] + counts)


def uneven(own_key, number_of, total, limit, lean):
    if number_of == 2:
        one = jax.random.randint(own_key, (), max(1, total - limit), min(limit, total - 1) + 1)
        return jnp.stack([one, total - one])
    tallies = jnp.asarray(length_profile(number_of, total, limit, lean), jnp.int32)
    pairs = (number_of - 1) // 2
    source_of, sink = tallies[1:1 + 2 * pairs:2], tallies[2:2 + 2 * pairs:2]
    room = jnp.minimum(source_of - 1, limit - sink)
    shifted = jax.random.randint(jax.random.fold_in(own_key, 1), (pairs,), 0, 1 << 20) % (room + 1)
    tallies = tallies.at[1:1 + 2 * pairs:2].set(source_of - shifted).at[2:2 + 2 * pairs:2].set(sink + shifted)
    return tallies[jax.random.permutation(jax.random.fold_in(own_key, 2), number_of)]


def noise(key, extent, spread, limit, cuts=(), kind=jnp.bfloat16):
    entries = jax.random.normal(key, extent, jnp.float32) * spread
    if len(cuts) > 0:
        entries = level_of(key, extent, cuts, -0.22, 0.18) * entries
    return jnp.clip(entries, min=-limit, max=limit).astype(kind)


def setup_inputs(seed: int = 0) -> dict:
    key_of = jax.random.split(jax.random.key(seed), 22)
    hidden_in = noise(key_of[0], (ROWS, ROW_LEN, D), 1.0, 6.0, ((0, 8), (1, 4)))
    out_grad = noise(key_of[1], (ROWS, ROW_LEN, D), 1.0, 6.0, ((0, 8), (1, 4)))
    doc_lengths = jax.vmap(lambda own: uneven(own, NDOC, ROW_LEN, DOC_MOST, 2))(jax.random.split(key_of[2], ROWS)).reshape((ROWS, NDOC)).astype(jnp.int32)
    norm_gains = jnp.clip(1.0 + 0.1 * jax.random.normal(key_of[3], (2, D), jnp.float32), 0.5, 1.5)
    w_query = noise(key_of[4], (D, H * HD), D ** -0.5, 0.125, ((0, 8), (1, 4)), jnp.float32)
    w_keyval = noise(key_of[5], (2, D, KV * HD), D ** -0.5, 0.125, ((1, 8), (2, 4)), jnp.float32)
    w_out = noise(key_of[6], (H * HD, D), (H * HD // 64) ** -0.5, 1.0, ((0, 4), (1, 8)), jnp.float32)
    w_gateup = noise(key_of[7], (2, D, FF), D ** -0.5, 0.125, ((1, 8), (2, 4)), jnp.float32)
    w_down = noise(key_of[8], (FF, D), FF ** -0.5, 0.0625, ((0, 4), (1, 8)), jnp.float32)
    moment_gains = noise(key_of[9], (2, D), (1.2 * TOKENS ** 0.5), 448.0, (), jnp.float32)
    moment_query = noise(key_of[10], (D, H * HD), (0.5 * TOKENS ** 0.5), 192.0, ((0, 8), (1, 4)), jnp.float32)
    moment_keyval = noise(key_of[11], (2, D, KV * HD), (0.7 * TOKENS ** 0.5), 256.0, ((1, 8), (2, 4)), jnp.float32)
    moment_out = noise(key_of[12], (H * HD, D), (0.15 * TOKENS ** 0.5), 56.0, ((0, 4), (1, 8)), jnp.float32)
    moment_gateup = noise(key_of[13], (2, D, FF), (0.5 * TOKENS ** 0.5), 192.0, ((1, 8), (2, 4)), jnp.float32)
    moment_down = noise(key_of[14], (FF, D), (0.6 * TOKENS ** 0.5), 224.0, ((0, 4), (1, 8)), jnp.float32)
    second_gains = jnp.clip(jnp.exp(jax.random.uniform(key_of[15], (2, D), jnp.float32, math.log(5898.24), math.log(23592.96))), 5898.24, 23592.96)
    second_query = jnp.clip(jnp.exp(math.log(4096.0) - 1.3862944 * jax.random.uniform(key_of[16], (D, H * HD), jnp.float32) ** level_of(key_of[16], (D, H * HD), ((0, 8), (1, 4)), -0.2, 0.2)), 1024.0, 4096.0)
    second_keyval = jnp.clip(jnp.exp(math.log(8028.16) - 1.3862944 * jax.random.uniform(key_of[17], (2, D, KV * HD), jnp.float32) ** level_of(key_of[17], (2, D, KV * HD), ((1, 8), (2, 4)), -0.2, 0.2)), 2007.04, 8028.16)
    second_out = jnp.clip(jnp.exp(math.log(368.64) - 1.3862944 * jax.random.uniform(key_of[18], (H * HD, D), jnp.float32) ** level_of(key_of[18], (H * HD, D), ((0, 4), (1, 8)), -0.2, 0.2)), 92.16, 368.64)
    second_gateup = jnp.clip(jnp.exp(math.log(4096.0) - 1.3862944 * jax.random.uniform(key_of[19], (2, D, FF), jnp.float32) ** level_of(key_of[19], (2, D, FF), ((1, 8), (2, 4)), -0.2, 0.2)), 1024.0, 4096.0)
    second_down = jnp.clip(jnp.exp(math.log(5898.24) - 1.3862944 * jax.random.uniform(key_of[20], (FF, D), jnp.float32) ** level_of(key_of[20], (FF, D), ((0, 4), (1, 8)), -0.2, 0.2)), 1474.56, 5898.24)
    return {"hidden_in": hidden_in, "out_grad": out_grad, "doc_lengths": doc_lengths, "norm_gains": norm_gains, "w_query": w_query, "w_keyval": w_keyval, "w_out": w_out, "w_gateup": w_gateup, "w_down": w_down, "moment_gains": moment_gains, "moment_query": moment_query, "moment_keyval": moment_keyval, "moment_out": moment_out, "moment_gateup": moment_gateup, "moment_down": moment_down, "second_gains": second_gains, "second_query": second_query, "second_keyval": second_keyval, "second_out": second_out, "second_gateup": second_gateup, "second_down": second_down}


EPS_NORM = 1e-05
BETA = 0.5
LAMB_EPS = 1e-06
DECAY = 0.01
RATE = 0.5
NEG_FILL = -1e+30
HIGHEST = lax.Precision.HIGHEST

@jax.custom_vjp
def low(v):
    return lax.optimization_barrier(v.astype(jnp.bfloat16)).astype(jnp.float32)

@jax.custom_vjp
def low_back(v):
    return v

def low_keep(v):
    return (low(v), None)

def low_pass(kept, grad):
    return (grad,)

def back_keep(v):
    return (v, None)

def back_low(kept, grad):
    return (low(grad),)
low.defvjp(low_keep, low_pass)
low_back.defvjp(back_keep, back_low)

def rope_inverse(half_dim):
    exponent = np.arange(half_dim, dtype=np.float32) * np.float32(2.0 / (2 * half_dim))
    base_freq = np.float32(1.0) / np.power(np.float32(500000.0), exponent)
    wave_len = np.float32(2.0 * np.pi) / base_freq
    smooth = (np.float32(8192.0) / wave_len - np.float32(1.0)) / np.float32(3.0)
    middle = (np.float32(1.0) - smooth) * base_freq / np.float32(32.0) + smooth * base_freq
    scaled = np.where(wave_len < 2048.0, base_freq, np.where(wave_len > 8192.0, base_freq / np.float32(32.0), middle))
    return scaled.astype(np.float32)

def doc_layout(lengths, row_len):
    doc_ends = jnp.cumsum(lengths, dtype=jnp.int32)
    starts_at = doc_ends - lengths
    position = jnp.arange(row_len, dtype=jnp.int32)
    segment = lax.optimization_barrier(jnp.sum((position[:, None] >= doc_ends[None, :]).astype(jnp.int32), axis=1, dtype=jnp.int32))
    onehot_doc = (segment[:, None] == jnp.arange(lengths.shape[0], dtype=jnp.int32)[None, :]).astype(jnp.int32)
    doc_place = position - lax.optimization_barrier(jnp.sum(onehot_doc * starts_at[None, :], axis=1, dtype=jnp.int32))
    return (segment, doc_place)

def rope_tables(doc_place, head_dim):
    inverse = jnp.asarray(rope_inverse(head_dim // 2))
    angles = doc_place.astype(jnp.float32)[:, None] * inverse[None, :]
    return (jnp.cos(angles), jnp.sin(angles))

def rotate(vectors, cosine, sine_part):
    half_dim = vectors.shape[-1] // 2
    front_half = vectors[..., :half_dim]
    back_half = vectors[..., half_dim:]
    cos_wide = cosine[:, None, :]
    sin_wide = sine_part[:, None, :]
    return jnp.concatenate([front_half * cos_wide - back_half * sin_wide, back_half * cos_wide + front_half * sin_wide], axis=-1)

def matmul(left_side, right_side):
    return jnp.dot(left_side, right_side, precision=HIGHEST)

def pair_sums(left_parts, right_parts):
    pieces = []
    for left_side, right_side, stacked in zip(left_parts, right_parts, (False, True, False, True, False)):
        product = left_side * right_side
        if stacked:
            pieces.append(lax.optimization_barrier(jnp.sum(product, axis=(1, 2))))
        else:
            pieces.append(jnp.sum(product)[None])
    return jnp.concatenate(pieces)

def scale_parts(parts, factors):
    return (parts[0] * factors[0], parts[1] * factors[1:3][:, None, None], parts[2] * factors[3], parts[3] * factors[4:6][:, None, None], parts[4] * factors[6])

def lamb_moments(gradient, moment, second):
    new_moment = BETA * moment + (1.0 - BETA) * gradient
    new_second = BETA * second + (1.0 - BETA) * gradient * gradient
    return (new_moment, new_second, new_moment / (jnp.sqrt(new_second) + LAMB_EPS))

def row_forward(weights, row_input, lengths):
    norm_gains, w_query, w_keyval, w_out, w_gateup, w_down = weights
    segment, doc_place = doc_layout(lengths, ROW_LEN)
    cosine, sine_part = rope_tables(doc_place, HD)
    inv_one = lax.rsqrt(lax.optimization_barrier(jnp.mean(row_input * row_input, axis=-1, keepdims=True)) + EPS_NORM)
    attn_input = low(row_input * inv_one * norm_gains[0])
    queries = low(rotate(low_back(matmul(attn_input, w_query)).reshape(ROW_LEN, H, HD), cosine, sine_part))
    key_rot = low(rotate(low_back(matmul(attn_input, w_keyval[0])).reshape(ROW_LEN, KV, HD), cosine, sine_part))
    values = low(low_back(matmul(attn_input, w_keyval[1]))).reshape(ROW_LEN, KV, HD)
    block_rows = min(512, ROW_LEN)
    count_blocks = ROW_LEN // block_rows
    group_size = H // KV
    score_scale = HD ** (-0.5)
    key_pos = jnp.arange(ROW_LEN, dtype=jnp.int32)

    def attend(block_index):
        first_row = block_index * block_rows
        query_block = lax.dynamic_slice_in_dim(queries, first_row, block_rows, 0).reshape(block_rows, KV, group_size, HD)
        seg_block = lax.dynamic_slice_in_dim(segment, first_row, block_rows, 0)
        pos_block = first_row + jnp.arange(block_rows, dtype=jnp.int32)
        allowed = (seg_block[:, None] == segment[None, :]) & (key_pos[None, :] <= pos_block[:, None])
        raw_scores = low_back(jnp.einsum('qkgd,tkd->kgqt', query_block, key_rot, precision=HIGHEST))
        scores = jnp.where(allowed[None, None], raw_scores * score_scale, NEG_FILL)
        probabilities = low(jax.nn.softmax(scores, axis=-1))
        context_block = jnp.einsum('kgqt,tkd->qkgd', probabilities, values, precision=HIGHEST)
        return context_block.reshape(block_rows, H * HD)
    blocks = lax.map(jax.checkpoint(attend), jnp.arange(count_blocks, dtype=jnp.int32))
    context = low(low_back(blocks.reshape(ROW_LEN, H * HD)))
    mid_stream = row_input + low_back(matmul(context, w_out))
    inv_two = lax.rsqrt(lax.optimization_barrier(jnp.mean(mid_stream * mid_stream, axis=-1, keepdims=True)) + EPS_NORM)
    ffn_input = low(mid_stream * inv_two * norm_gains[1])
    gate_pre = low_back(matmul(ffn_input, w_gateup[0]))
    up_pre = low_back(matmul(ffn_input, w_gateup[1]))
    hidden_act = low(jax.nn.silu(gate_pre) * up_pre)
    return mid_stream + low_back(matmul(hidden_act, w_down))

def reference(hidden_in, out_grad, doc_lengths, norm_gains, w_query, w_keyval, w_out, w_gateup, w_down, moment_gains, moment_query, moment_keyval, moment_out, moment_gateup, moment_down, second_gains, second_query, second_keyval, second_out, second_gateup, second_down):
    params = (norm_gains, w_query, w_keyval, w_out, w_gateup, w_down)
    group_rows = math.gcd(ROWS, max(1, 4096 // ROW_LEN))
    count_groups = ROWS // group_rows

    def forward(weights, block_input, block_lengths):
        rounded = (weights[0],) + tuple((low(matrix) for matrix in weights[1:]))
        return jax.vmap(lambda row_input, lengths: row_forward(rounded, row_input, lengths))(block_input, block_lengths)

    def group_step(running, inputs):
        block_input, block_cot, block_lengths = inputs
        outputs, pullback = jax.vjp(lambda weights, data: forward(weights, data, block_lengths), params, block_input.astype(jnp.float32))
        grad_weights, grad_data = pullback(block_cot.astype(jnp.float32))
        running = jax.tree.map(lambda before, after: before + after, running, grad_weights)
        return (running, (outputs.astype(jnp.bfloat16), grad_data))
    zero_grads = jax.tree.map(lambda array: jnp.zeros(array.shape, jnp.float32), params)
    inputs = (hidden_in.reshape(count_groups, group_rows, ROW_LEN, D), out_grad.reshape(count_groups, group_rows, ROW_LEN, D), doc_lengths.reshape(count_groups, group_rows, NDOC))
    grads, (outputs, grad_data) = lax.scan(group_step, zero_grads, inputs)
    block_out = outputs.reshape(ROWS, ROW_LEN, D)
    input_grad = grad_data.reshape(ROWS, ROW_LEN, D)
    grad_gains = grads[0]
    grad_parts = grads[1:]
    masters = (w_query, w_keyval, w_out, w_gateup, w_down)
    moments = (moment_query, moment_keyval, moment_out, moment_gateup, moment_down)
    seconds = (second_query, second_keyval, second_out, second_gateup, second_down)
    results = [lamb_moments(grad_parts[slot], moments[slot], seconds[slot]) for slot in range(5)]
    new_moments = tuple((entry[0] for entry in results))
    new_seconds = tuple((entry[1] for entry in results))
    updates = tuple((results[slot][2] + DECAY * masters[slot] for slot in range(5)))
    gain_moment, gain_second, gain_direction = lamb_moments(grad_gains, moment_gains, second_gains)
    gain_update = gain_direction + DECAY * norm_gains
    weight_norms = jnp.concatenate([jnp.sqrt(pair_sums(masters, masters)), jnp.sqrt(lax.optimization_barrier(jnp.sum(norm_gains * norm_gains, axis=1)))])
    update_norms = jnp.concatenate([jnp.sqrt(pair_sums(updates, updates)), jnp.sqrt(lax.optimization_barrier(jnp.sum(gain_update * gain_update, axis=1)))])
    trust_ratios = weight_norms / update_norms
    steps_taken = scale_parts(updates, trust_ratios[:7])
    new_parts = tuple((masters[slot] - RATE * steps_taken[slot] for slot in range(5)))
    new_gains = norm_gains - RATE * trust_ratios[7:9][:, None] * gain_update
    return (block_out, input_grad, grad_gains, grad_parts[0], grad_parts[1], grad_parts[2], grad_parts[3], grad_parts[4], new_gains, new_parts[0], new_parts[1], new_parts[2], new_parts[3], new_parts[4], gain_moment, new_moments[0], new_moments[1], new_moments[2], new_moments[3], new_moments[4], gain_second, new_seconds[0], new_seconds[1], new_seconds[2], new_seconds[3], new_seconds[4], weight_norms, update_norms, trust_ratios)
```

```python
import jax
import jax.numpy as jnp
import numpy as np
from jax import lax
from jax.sharding import PartitionSpec as P

HD = 64


EPS_NORM = 1e-05
BETA = 0.5
LAMB_EPS = 1e-06
DECAY = 0.01
RATE = 0.5
NEG_FILL = -1e30


def rope_inverse(half_dim):
    exponent = np.arange(half_dim, dtype=np.float32) * np.float32(2.0 / (2 * half_dim))
    base_freq = np.float32(1.0) / np.power(np.float32(500000.0), exponent)
    wave_len = np.float32(2.0 * np.pi) / base_freq
    smooth = (np.float32(8192.0) / wave_len - np.float32(1.0)) / np.float32(3.0)
    middle = (np.float32(1.0) - smooth) * base_freq / np.float32(32.0) + smooth * base_freq
    scaled = np.where(
        wave_len < 2048.0,
        base_freq,
        np.where(wave_len > 8192.0, base_freq / np.float32(32.0), middle),
    )
    return scaled.astype(np.float32)


def doc_layout(lengths, position):
    doc_ends = jnp.cumsum(lengths, dtype=jnp.int32)
    starts_at = doc_ends - lengths
    segment = jnp.sum(
        (position[:, None] >= doc_ends[None, :]).astype(jnp.int32), axis=1, dtype=jnp.int32
    )
    onehot_doc = (
        segment[:, None] == jnp.arange(lengths.shape[0], dtype=jnp.int32)[None, :]
    ).astype(jnp.int32)
    doc_place = position - jnp.sum(onehot_doc * starts_at[None, :], axis=1, dtype=jnp.int32)
    return (segment, doc_place)


def rope_tables(doc_place, head_dim):
    inverse = jnp.asarray(rope_inverse(head_dim // 2))
    angles = doc_place.astype(jnp.float32)[:, None] * inverse[None, :]
    return (jnp.cos(angles), jnp.sin(angles))


def rotate(vectors, cosine, sine_part):
    half_dim = vectors.shape[-1] // 2
    front_half = vectors[..., :half_dim]
    back_half = vectors[..., half_dim:]
    cos_wide = cosine[:, None, :]
    sin_wide = sine_part[:, None, :]
    return jnp.concatenate(
        [
            front_half * cos_wide - back_half * sin_wide,
            back_half * cos_wide + front_half * sin_wide,
        ],
        axis=-1,
    )


def unrotate(gradient, cosine, sine_part):
    half_dim = gradient.shape[-1] // 2
    front_half = gradient[..., :half_dim]
    back_half = gradient[..., half_dim:]
    cos_wide = cosine[:, None, :]
    sin_wide = sine_part[:, None, :]
    return jnp.concatenate(
        [
            front_half * cos_wide + back_half * sin_wide,
            back_half * cos_wide - front_half * sin_wide,
        ],
        axis=-1,
    )


def rounded(value):
    return value.astype(jnp.bfloat16)


def widened(value):
    return value.astype(jnp.float32)


def dot_plain(left_side, right_side):
    return jnp.dot(left_side, right_side, preferred_element_type=jnp.float32)


def dot_rows(left_side, right_side):
    return lax.dot_general(
        left_side, right_side, (((1,), (1,)), ((), ())), preferred_element_type=jnp.float32
    )


def dot_cols(left_side, right_side):
    return lax.dot_general(
        left_side, right_side, (((0,), (0,)), ((), ())), preferred_element_type=jnp.float32
    )


def exchange(value, axis, mask):
    if isinstance(axis, tuple):
        size = 1
        for name in axis:
            size = size * lax.axis_size(name)
    else:
        size = lax.axis_size(axis)
    return lax.ppermute(value, axis, [(place, place ^ mask) for place in range(size)])


def gather_row(value):
    pair = jnp.concatenate([value, exchange(value, "y", 1)])
    return jnp.concatenate([pair, exchange(pair, "c", 1)])


def scatter_row(partial):
    half = partial.shape[0] // 2
    quarter = half // 2
    summed = widened(partial[:half]) + widened(exchange(partial[half:], "c", 1))
    return summed[:quarter] + widened(exchange(rounded(summed[quarter:]), "y", 1))


def all_sum(value):
    for axis in ("c", "y", "x", "z", "o"):
        mask = 1
        while mask < lax.axis_size(axis):
            value = value + exchange(value, axis, mask)
            mask = mask * 2
    return value


def lamb_moments(gradient, moment, second):
    new_moment = BETA * moment + (1.0 - BETA) * gradient
    new_second = BETA * second + (1.0 - BETA) * gradient * gradient
    return (new_moment, new_second, new_moment / (jnp.sqrt(new_second) + LAMB_EPS))


def square_sums(parts):
    pieces = []
    for part, stacked in zip(parts, (False, True, False, True, False)):
        if stacked:
            pieces.append(jnp.sum(part[0] * part[0]))
            pieces.append(jnp.sum(part[1] * part[1]))
        else:
            pieces.append(jnp.sum(part * part))
    return jnp.stack(pieces)


def scale_parts(parts, factors):
    return (
        parts[0] * factors[0],
        parts[1] * factors[1:3][:, None, None],
        parts[2] * factors[3],
        parts[3] * factors[4:6][:, None, None],
        parts[4] * factors[6],
    )


def per_device(
    hidden_in,
    out_grad,
    doc_lengths,
    norm_gains,
    w_query,
    w_keyval,
    w_out,
    w_gateup,
    w_down,
    moment_gains,
    moment_query,
    moment_keyval,
    moment_out,
    moment_gateup,
    moment_down,
    second_gains,
    second_query,
    second_keyval,
    second_out,
    second_gateup,
    second_down,
):
    tok = hidden_in.shape[1]
    width = hidden_in.shape[2]
    row_len = tok * 4
    n_o, n_z, n_x = lax.axis_size("o"), lax.axis_size("z"), lax.axis_size("x")
    n_parts = n_o * n_x
    depth = w_query.shape[0]
    part_depth = n_z * depth
    heads_wide = w_query.shape[1]
    kv_wide = w_keyval.shape[2]
    local_heads = heads_wide // HD
    local_kv = kv_wide // HD
    group_size = local_heads // local_kv
    ff_held = w_down.shape[0]
    ff_part = ff_held // n_z
    score_scale = HD ** (-0.5)
    my_part = lax.axis_index("o") * n_x + lax.axis_index("x")

    def to_parts(value):
        cut = value.reshape(tok, n_o, n_z, n_x, depth).transpose(1, 3, 0, 2, 4)
        cut = cut.reshape(n_parts, tok, part_depth)
        return jnp.concatenate(
            [
                lax.dynamic_index_in_dim(cut, my_part ^ place, 0, keepdims=False)
                for place in range(n_parts)
            ],
            axis=1,
        )

    def from_parts(value):
        cut = value.reshape(tok, n_parts, part_depth)
        cut = jnp.stack(
            [
                lax.dynamic_index_in_dim(cut, my_part ^ place, 1, keepdims=False)
                for place in range(n_parts)
            ]
        )
        cut = cut.reshape(n_o, n_x, tok, n_z, depth).transpose(2, 0, 3, 1, 4)
        return cut.reshape(tok, width)

    def gather_rows(value):
        return jnp.concatenate(
            [gather_row(exchange(value, "z", place) if place else value) for place in range(n_z)]
        )

    def scatter_rows(partials):
        total = None
        for place in range(n_z - 1, -1, -1):
            mine = scatter_row(partials[place])
            if place:
                mine = widened(exchange(rounded(mine), "z", place))
            total = mine if total is None else total + mine
        return total

    masters = (w_query, w_keyval, w_out, w_gateup, w_down)
    y_at, c_at = lax.axis_index("y"), lax.axis_index("c")
    token_blocks = [
        ((y_at ^ y_other) * 2 + (c_at ^ c_other)) * tok + jnp.arange(tok, dtype=jnp.int32)
        for c_other in range(2)
        for y_other in range(2)
    ]
    position = jnp.concatenate(token_blocks)
    segment, doc_place = doc_layout(doc_lengths[0], position)
    cosine, sine_part = rope_tables(doc_place, HD)

    attn_shard = rounded(jnp.concatenate([w_query, w_keyval[0], w_keyval[1], w_out.T], axis=1))
    attn_w = lax.all_gather(attn_shard, ("o", "z", "x"), axis=0, tiled=True)
    qkv_wide = heads_wide + 2 * kv_wide
    qkv_w, out_wt = attn_w[:, :qkv_wide], attn_w[:, qkv_wide:]

    gateup_send = rounded(w_gateup).reshape(2, depth, n_z, ff_part).transpose(2, 1, 0, 3)
    gateup_own = lax.all_to_all(
        gateup_send.reshape(n_z, depth, 2 * ff_part), "z", 0, 0, tiled=True
    ).reshape(part_depth, 2 * ff_part)
    down_own = lax.all_to_all(
        rounded(w_down).reshape(n_z, ff_part, depth), "z", 0, 0, tiled=True
    )
    gateup_w = jnp.concatenate(
        [
            exchange(gateup_own, ("o", "x"), place) if place else gateup_own
            for place in range(n_parts)
        ]
    )
    down_w = jnp.concatenate(
        [
            exchange(down_own, ("o", "x"), place) if place else down_own
            for place in range(n_parts)
        ]
    )
    down_w = down_w.transpose(1, 0, 2).reshape(ff_part, width)

    x_float = widened(hidden_in[0])
    gain_attn = norm_gains[0]
    gain_ffn = norm_gains[1]
    inv_one = lax.rsqrt(jnp.mean(x_float * x_float, axis=-1, keepdims=True) + EPS_NORM)
    normed_one = x_float * inv_one
    attn_input = gather_row(rounded(normed_one * gain_attn))
    qkv = dot_plain(attn_input, qkv_w)
    query_raw = qkv[:, :heads_wide].reshape(row_len, local_heads, HD)
    key_raw = qkv[:, heads_wide : heads_wide + kv_wide].reshape(row_len, local_kv, HD)
    values = rounded(qkv[:, heads_wide + kv_wide :]).reshape(row_len, local_kv, HD)
    queries = rounded(rotate(query_raw, cosine, sine_part)).reshape(
        row_len, local_kv, group_size, HD
    )
    key_rot = rounded(rotate(key_raw, cosine, sine_part))
    allowed = (segment[:, None] == segment[None, :]) & (position[None, :] <= position[:, None])
    scores = jnp.where(
        allowed[None, None],
        jnp.einsum("qkgd,tkd->kgqt", queries, key_rot, preferred_element_type=jnp.float32)
        * score_scale,
        NEG_FILL,
    )
    row_max = jnp.max(scores, axis=-1, keepdims=True)
    shifted = jnp.exp(scores - row_max)
    probabilities = shifted / jnp.sum(shifted, axis=-1, keepdims=True)
    prob_round = rounded(probabilities)
    context = rounded(
        jnp.einsum("kgqt,tkd->qkgd", prob_round, values, preferred_element_type=jnp.float32)
    ).reshape(row_len, heads_wide)
    mid_stream = x_float + scatter_row(rounded(dot_rows(context, out_wt)))
    inv_two = lax.rsqrt(jnp.mean(mid_stream * mid_stream, axis=-1, keepdims=True) + EPS_NORM)
    normed_two = mid_stream * inv_two

    ffn_input = gather_rows(to_parts(rounded(normed_two * gain_ffn)))
    grad_full = gather_rows(to_parts(out_grad[0]))
    gateup_pre = dot_plain(ffn_input, gateup_w)
    gate_pre, up_pre = gateup_pre[:, :ff_part], gateup_pre[:, ff_part:]
    sigmoid_gate = jax.nn.sigmoid(gate_pre)
    silu_gate = gate_pre * sigmoid_gate
    hidden_act = rounded(silu_gate * up_pre)
    ffn_out = scatter_rows(
        [
            rounded(dot_plain(hidden_act[place * row_len : (place + 1) * row_len], down_w))
            for place in range(n_z)
        ]
    )
    block_out = rounded(mid_stream + from_parts(ffn_out))[None]

    grad_hidden = dot_rows(grad_full, down_w)
    grad_gate = grad_hidden * up_pre * (sigmoid_gate * (1.0 + gate_pre * (1.0 - sigmoid_gate)))
    grad_up = grad_hidden * silu_gate
    grad_pair = jnp.concatenate([rounded(grad_gate), rounded(grad_up)], axis=1)
    grad_ffn_in = from_parts(
        scatter_rows(
            [
                rounded(dot_rows(grad_pair[place * row_len : (place + 1) * row_len], gateup_w))
                for place in range(n_z)
            ]
        )
    )
    grad_gateup_w = dot_cols(ffn_input, grad_pair).reshape(n_parts, n_z, depth, 2 * ff_part)
    grad_down_w = dot_cols(hidden_act, grad_full).reshape(ff_part, n_parts, n_z, depth)

    def to_owner(pieces):
        total = pieces[0]
        for place in range(1, n_parts):
            total = total + widened(exchange(rounded(pieces[place]), ("o", "x"), place))
        return widened(lax.all_to_all(rounded(total), "z", 0, 0, tiled=True))

    grad_gateup = (
        to_owner([grad_gateup_w[place] for place in range(n_parts)])
        .reshape(n_z, depth, 2, ff_part)
        .transpose(2, 1, 0, 3)
        .reshape(2, depth, ff_held)
    )
    grad_down = to_owner(
        [grad_down_w[:, place].transpose(1, 0, 2) for place in range(n_parts)]
    ).reshape(ff_held, depth)

    gain_grad_ffn = jnp.sum(grad_ffn_in * normed_two, axis=0)
    grad_normed_two = grad_ffn_in * gain_ffn
    grad_mid = widened(out_grad[0]) + inv_two * (
        grad_normed_two
        - normed_two * jnp.mean(grad_normed_two * normed_two, axis=-1, keepdims=True)
    )
    grad_mid_full = gather_row(rounded(grad_mid))
    grad_context = rounded(dot_plain(grad_mid_full, out_wt)).reshape(
        row_len, local_kv, group_size, HD
    )
    grad_out_wt = rounded(dot_cols(grad_mid_full, context))
    grad_out = widened(
        lax.psum_scatter(grad_out_wt, ("o", "z", "x"), scatter_dimension=0, tiled=True)
    ).T

    grad_probs = jnp.einsum(
        "qkgd,tkd->kgqt", grad_context, values, preferred_element_type=jnp.float32
    )
    inner_sum = jnp.sum(probabilities * grad_probs, axis=-1, keepdims=True)
    grad_scores = rounded(probabilities * (grad_probs - inner_sum) * score_scale)
    grad_queries = jnp.einsum(
        "kgqt,tkd->qkgd", grad_scores, key_rot, preferred_element_type=jnp.float32
    ).reshape(row_len, local_heads, HD)
    grad_keys = jnp.einsum(
        "kgqt,qkgd->tkd", grad_scores, queries, preferred_element_type=jnp.float32
    )
    grad_values = jnp.einsum(
        "kgqt,qkgd->tkd", prob_round, grad_context, preferred_element_type=jnp.float32
    )
    grad_qkv = jnp.concatenate(
        [
            rounded(unrotate(grad_queries, cosine, sine_part)).reshape(row_len, heads_wide),
            rounded(unrotate(grad_keys, cosine, sine_part)).reshape(row_len, kv_wide),
            rounded(grad_values).reshape(row_len, kv_wide),
        ],
        axis=1,
    )
    grad_qkv_w = widened(
        lax.psum_scatter(
            rounded(dot_cols(attn_input, grad_qkv)),
            ("o", "z", "x"),
            scatter_dimension=0,
            tiled=True,
        )
    )
    grad_query = grad_qkv_w[:, :heads_wide]
    grad_keyval = jnp.stack(
        [
            grad_qkv_w[:, heads_wide : heads_wide + kv_wide],
            grad_qkv_w[:, heads_wide + kv_wide :],
        ]
    )
    grad_attn_in = scatter_row(rounded(dot_rows(grad_qkv, qkv_w)))
    gain_grad_attn = jnp.sum(grad_attn_in * normed_one, axis=0)
    grad_normed_one = grad_attn_in * gain_attn
    input_grad = grad_mid + inv_one * (
        grad_normed_one
        - normed_one * jnp.mean(grad_normed_one * normed_one, axis=-1, keepdims=True)
    )

    grad_parts = (grad_query, grad_keyval, grad_out, grad_gateup, grad_down)
    moments = (moment_query, moment_keyval, moment_out, moment_gateup, moment_down)
    seconds = (second_query, second_keyval, second_out, second_gateup, second_down)
    results = [lamb_moments(grad_parts[slot], moments[slot], seconds[slot]) for slot in range(5)]
    new_moments = tuple((entry[0] for entry in results))
    new_seconds = tuple((entry[1] for entry in results))
    updates = tuple((results[slot][2] + DECAY * masters[slot] for slot in range(5)))
    packed = jnp.concatenate(
        [gain_grad_attn, gain_grad_ffn, jnp.pad(square_sums(masters), (0, 121))]
    ).reshape(-1, 128)
    packed = all_sum(packed)
    grad_gains = packed[:-1].reshape(2, width)
    weight_sq = packed[-1, :7]
    update_sq = all_sum(jnp.pad(square_sums(updates), (0, 121)).reshape(1, 128))[0, :7]
    gain_moment, gain_second, gain_direction = lamb_moments(grad_gains, moment_gains, second_gains)
    gain_update = gain_direction + DECAY * norm_gains
    weight_norms = jnp.concatenate(
        [jnp.sqrt(weight_sq), jnp.sqrt(jnp.sum(norm_gains * norm_gains, axis=1))]
    )
    update_norms = jnp.concatenate(
        [jnp.sqrt(update_sq), jnp.sqrt(jnp.sum(gain_update * gain_update, axis=1))]
    )
    trust_ratios = weight_norms / update_norms
    steps_taken = scale_parts(updates, trust_ratios[:7])
    new_parts = tuple((masters[slot] - RATE * steps_taken[slot] for slot in range(5)))
    new_gains = norm_gains - RATE * trust_ratios[7:9][:, None] * gain_update
    return (
        block_out,
        input_grad[None],
        grad_gains,
        grad_parts[0],
        grad_parts[1],
        grad_parts[2],
        grad_parts[3],
        grad_parts[4],
        new_gains,
        new_parts[0],
        new_parts[1],
        new_parts[2],
        new_parts[3],
        new_parts[4],
        gain_moment,
        new_moments[0],
        new_moments[1],
        new_moments[2],
        new_moments[3],
        new_moments[4],
        gain_second,
        new_seconds[0],
        new_seconds[1],
        new_seconds[2],
        new_seconds[3],
        new_seconds[4],
        weight_norms,
        update_norms,
        trust_ratios,
    )


def solution(mesh):
    n_dp, n_tensor = mesh.devices.shape
    split = jax.sharding.Mesh(
        mesh.devices.reshape(n_dp // 8, 4, 2, n_tensor // 2, 2), ("o", "z", "x", "y", "c")
    )
    dp, tensor = ("o", "z", "x"), ("y", "c")
    in_specs = (
        P(dp, tensor, None),
        P(dp, tensor, None),
        P(dp, None),
        P(),
        P(dp, tensor),
        P(None, dp, tensor),
        P(tensor, dp),
        P(None, dp, tensor),
        P(tensor, dp),
        P(),
        P(dp, tensor),
        P(None, dp, tensor),
        P(tensor, dp),
        P(None, dp, tensor),
        P(tensor, dp),
        P(),
        P(dp, tensor),
        P(None, dp, tensor),
        P(tensor, dp),
        P(None, dp, tensor),
        P(tensor, dp),
    )
    out_specs = (
        P(dp, tensor, None),
        P(dp, tensor, None),
        P(),
        P(dp, tensor),
        P(None, dp, tensor),
        P(tensor, dp),
        P(None, dp, tensor),
        P(tensor, dp),
        P(),
        P(dp, tensor),
        P(None, dp, tensor),
        P(tensor, dp),
        P(None, dp, tensor),
        P(tensor, dp),
        P(),
        P(dp, tensor),
        P(None, dp, tensor),
        P(tensor, dp),
        P(None, dp, tensor),
        P(tensor, dp),
        P(),
        P(dp, tensor),
        P(None, dp, tensor),
        P(tensor, dp),
        P(None, dp, tensor),
        P(tensor, dp),
        P(),
        P(),
        P(),
    )
    return jax.shard_map(
        per_device, mesh=split, in_specs=in_specs, out_specs=out_specs, check_vma=False
    )
```

```python
import jax
import jax.numpy as jnp
import numpy as np
from jax import lax
from jax.experimental import pallas as pl
from jax.experimental.pallas import tpu as pltpu
from jax.sharding import PartitionSpec as P

HD = 64


EPS_NORM = 1e-05
BETA = 0.5
LAMB_EPS = 1e-06
DECAY = 0.01
RATE = 0.5
NEG_FILL = -1e30


def rope_inverse(half_dim):
    exponent = np.arange(half_dim, dtype=np.float32) * np.float32(2.0 / (2 * half_dim))
    base_freq = np.float32(1.0) / np.power(np.float32(500000.0), exponent)
    wave_len = np.float32(2.0 * np.pi) / base_freq
    smooth = (np.float32(8192.0) / wave_len - np.float32(1.0)) / np.float32(3.0)
    middle = (np.float32(1.0) - smooth) * base_freq / np.float32(32.0) + smooth * base_freq
    scaled = np.where(
        wave_len < 2048.0,
        base_freq,
        np.where(wave_len > 8192.0, base_freq / np.float32(32.0), middle),
    )
    return scaled.astype(np.float32)


def doc_layout(lengths, position):
    doc_ends = jnp.cumsum(lengths, dtype=jnp.int32)
    starts_at = doc_ends - lengths
    segment = jnp.sum(
        (position[:, None] >= doc_ends[None, :]).astype(jnp.int32), axis=1, dtype=jnp.int32
    )
    onehot_doc = (
        segment[:, None] == jnp.arange(lengths.shape[0], dtype=jnp.int32)[None, :]
    ).astype(jnp.int32)
    doc_place = position - jnp.sum(onehot_doc * starts_at[None, :], axis=1, dtype=jnp.int32)
    return (segment, doc_place)


def rope_tables(doc_place, head_dim):
    inverse = jnp.asarray(rope_inverse(head_dim // 2))
    angles = doc_place.astype(jnp.float32)[:, None] * inverse[None, :]
    return (jnp.cos(angles), jnp.sin(angles))


def rounded(value):
    return value.astype(jnp.bfloat16)


def widened(value):
    return value.astype(jnp.float32)


def dot_plain(left_side, right_side):
    return lax.dot_general(
        left_side, right_side, (((1,), (0,)), ((), ())), preferred_element_type=jnp.float32
    )


def dot_rows(left_side, right_side):
    return lax.dot_general(
        left_side, right_side, (((1,), (1,)), ((), ())), preferred_element_type=jnp.float32
    )


def dot_cols(left_side, right_side):
    return lax.dot_general(
        left_side, right_side, (((0,), (0,)), ((), ())), preferred_element_type=jnp.float32
    )


def exchange(value, axis, mask, what="swap"):
    names = axis if isinstance(axis, tuple) else (axis,)
    size = 1
    for name in names:
        size = size * lax.axis_size(name)
    with jax.named_scope(what):
        return lax.ppermute(value, axis, [(place, place ^ mask) for place in range(size)])


def resplit(value, what):
    with jax.named_scope(what):
        return lax.all_to_all(value, "z", 0, 0, tiled=True)


def after(value, *others):
    return lax.optimization_barrier((value,) + others)[0]


def gather_row(value, what):
    across = exchange(value, "y", 1, what + "_y")
    return gather_core(value, across, what)


def gather_core(value, across, what, *waits):
    pair = jnp.concatenate([value, after(across, *waits)])
    return (value, across, exchange(pair, "c", 1, what + "_c"))


class RowSum:
    def __init__(self, keep, send, what):
        self.keep, self.what = keep, what
        self.tokens = keep.shape[0] // 2
        self.received = exchange(send, "c", 1, what + "_c")

    def pass_on(self, *waits):
        tokens = self.tokens
        received = after(self.received, *waits)
        passed = rounded(widened(self.keep[tokens:]) + widened(received[tokens:]))
        self.across = exchange(passed, "y", 1, self.what + "_y")

    def total(self):
        tokens = self.tokens
        return (
            widened(self.keep[:tokens])
            + widened(self.received[:tokens])
            + widened(self.across)
        )


def scatter_row(keep, send, what):
    row = RowSum(keep, send, what)
    row.pass_on()
    return row.total()


def all_sum(value):
    for axis in ("c", "x", "y", "z", "o"):
        mask = 1
        while mask < lax.axis_size(axis):
            value = value + exchange(value, axis, mask)
            mask = mask * 2
    return value


HBM = pl.BlockSpec(memory_space=pl.ANY)
VMEM = pl.BlockSpec(memory_space=pltpu.VMEM)
SMEM = pl.BlockSpec(memory_space=pltpu.SMEM)


def start_copies(pairs, sems, first=0):
    copies = [
        pltpu.make_async_copy(source, target, sems.at[first + place])
        for place, (source, target) in enumerate(pairs)
    ]
    for copy in copies:
        copy.start()
    return copies


def row_copies(pieces, target):
    pairs, first = [], 0
    for piece in pieces:
        pairs.append((piece, target.at[pl.ds(first, piece.shape[0]), :]))
        first += piece.shape[0]
    return pairs


def block_rows_of(index, place, depth):
    return pl.ds(pl.multiple_of(index[place] * depth, depth), depth)


def lane_iota(rows):
    return lax.broadcasted_iota(jnp.int32, (rows, 128), 1)


def partner(value):
    lane = lane_iota(value.shape[0])
    return jnp.where(lane % HD < HD // 2, pltpu.roll(value, 128 - HD // 2, 1), pltpu.roll(value, HD // 2, 1))


def head_lanes(value, head, kv):
    lane = lane_iota(value.shape[0])
    moved = value if head % 2 == kv else pltpu.roll(value, HD, 1)
    keep = lane < HD if kv == 0 else lane >= HD
    return jnp.where(keep, moved, 0.0)


def pair_slab(even, odd, kv):
    lane = lane_iota(even.shape[0])
    if kv == 0:
        odd = pltpu.roll(odd, HD, 1)
    else:
        even = pltpu.roll(even, HD, 1)
    return jnp.where(lane < HD, even, odd)


CHUNK = 256


def attend_body(n_blocks, heads, group, *refs):
    index, a_own, a_across, a_core = refs[:4]
    weights = refs[4 : 4 + n_blocks]
    cosine, sine, bias = refs[4 + n_blocks : 7 + n_blocks]
    a_all, q_out, kv_out, ctx_out, lse_out = refs[7 + n_blocks : 12 + n_blocks]
    held, sems = refs[12 + n_blocks :]
    depth = weights[0].shape[0]
    copies = start_copies(row_copies((a_own, a_across, a_core), a_all), sems)
    copies += start_copies(
        [
            (weights[i].at[:, : held.shape[1]], held.at[block_rows_of(index, i, depth), :])
            for i in range(n_blocks)
        ],
        sems,
        3,
    )
    for copy in copies:
        copy.wait()
    rows_all = a_all.shape[0]
    n_slabs = heads // 2

    @pl.loop(0, rows_all // CHUNK)
    def _(at):
        rows = pl.ds(pl.multiple_of(at * CHUNK, CHUNK), CHUNK)
        raw = dot_plain(a_all[rows, :], held[...])
        cos, sin = cosine[rows, :], sine[rows, :]
        for slab in range(n_slabs + 1):
            part = raw[:, slab * 128 : (slab + 1) * 128]
            part = part * cos + partner(part) * sin
            if slab < n_slabs:
                for head in (2 * slab, 2 * slab + 1):
                    q_out[head, rows, :] = rounded(head_lanes(part, head, head // group))
            else:
                kv_out[0, rows, :] = rounded(part)
        kv_out[1, rows, :] = rounded(raw[:, (n_slabs + 1) * 128 : (n_slabs + 2) * 128])

    @pl.loop(0, rows_all // CHUNK)
    def _(at):
        rows = pl.ds(pl.multiple_of(at * CHUNK, CHUNK), CHUNK)
        keys, values = kv_out[0], kv_out[1]
        lane = lane_iota(CHUNK)
        logs = jnp.zeros((CHUNK, 128), jnp.float32)
        for slab in range(n_slabs):
            outs = []
            for head in (2 * slab, 2 * slab + 1):
                scores = dot_rows(q_out[head, rows, :], keys) * HD ** (-0.5) + bias[rows, :]
                most = jnp.max(scores, axis=-1, keepdims=True)
                shifted = jnp.exp(scores - most)
                total = jnp.sum(shifted, axis=-1, keepdims=True)
                outs.append(dot_plain(rounded(shifted / total), values))
                logs = jnp.where(lane == head, most + jnp.log(total), logs)
            ctx_out[rows, slab * 128 : (slab + 1) * 128] = rounded(
                pair_slab(outs[0], outs[1], 2 * slab // group)
            )
        lse_out[rows, :] = logs


def attend_back_body(n_blocks, heads, group, *refs):
    index, d_all = refs[:2]
    weights = refs[2 : 2 + n_blocks]
    queries, keyvals, bias, logs, cosine, sine = refs[2 + n_blocks : 8 + n_blocks]
    out = refs[8 + n_blocks]
    held, d_heads, key_sum, value_sum, sems = refs[9 + n_blocks :]
    depth, wide = weights[0].shape[0], held.shape[1]
    first = weights[0].shape[1] - wide
    copies = start_copies(
        [
            (weights[i].at[:, pl.ds(first, wide)], held.at[block_rows_of(index, i, depth), :])
            for i in range(n_blocks)
        ],
        sems,
    )
    for copy in copies:
        copy.wait()
    rows_all = d_all.shape[0]
    n_slabs = heads // 2
    key_sum[...] = jnp.zeros_like(key_sum)
    value_sum[...] = jnp.zeros_like(value_sum)

    @pl.loop(0, rows_all // CHUNK)
    def _(at):
        rows = pl.ds(pl.multiple_of(at * CHUNK, CHUNK), CHUNK)
        d_ctx = dot_plain(d_all[rows, :], held[...])
        for slab in range(n_slabs):
            part = d_ctx[:, slab * 128 : (slab + 1) * 128]
            for head in (2 * slab, 2 * slab + 1):
                d_heads[head, :, :] = rounded(head_lanes(part, head, head // group))
        keys, values = keyvals[0], keyvals[1]
        lane = lane_iota(CHUNK)
        cos, sin = cosine[rows, :], sine[rows, :]
        log_rows = logs[rows, :]
        for slab in range(n_slabs):
            kv = 2 * slab // group
            outs = []
            for head in (2 * slab, 2 * slab + 1):
                query, d_head = queries[head, rows, :], d_heads[head]
                log_total = jnp.sum(jnp.where(lane == head, log_rows, 0.0), axis=-1, keepdims=True)
                scores = dot_rows(query, keys) * HD ** (-0.5) + bias[rows, :]
                probs = jnp.exp(scores - log_total)
                d_probs = dot_rows(d_head, values)
                inner = jnp.sum(probs * d_probs, axis=-1, keepdims=True)
                d_scores = rounded(probs * (d_probs - inner) * HD ** (-0.5))
                key_sum[...] += dot_cols(d_scores, query)
                value_sum[...] += dot_cols(rounded(probs), d_head)
                outs.append(dot_plain(d_scores, keys))
            part = pair_slab(outs[0], outs[1], kv)
            out[rows, slab * 128 : (slab + 1) * 128] = rounded(part * cos - partner(part) * sin)

    key_grad = key_sum[...]
    key_grad = key_grad * cosine[...] - partner(key_grad) * sine[...]
    out[:, n_slabs * 128 : (n_slabs + 1) * 128] = rounded(key_grad)
    out[:, (n_slabs + 1) * 128 : (n_slabs + 2) * 128] = rounded(value_sum[...])


def rows_out_body(n_blocks, first, *refs):
    index, left = refs[:2]
    weights = refs[2 : 2 + n_blocks]
    keep, send, held, sems = refs[2 + n_blocks :]
    depth, wide = weights[0].shape[0], held.shape[1]
    copies = start_copies(
        [
            (weights[i].at[:, pl.ds(first, wide)], held.at[block_rows_of(index, i, depth), :])
            for i in range(n_blocks)
        ],
        sems,
    )
    for copy in copies:
        copy.wait()
    half = left.shape[0] // 2
    send[...] = rounded(dot_rows(left[half:, :], held[...]))
    keep[...] = rounded(dot_rows(left[:half, :], held[...]))


def natural_rows(scalars, pieces, which, target):
    tokens = pieces[0].shape[0] // 2
    pairs = []
    for at in range(4):
        place = pl.ds(pl.multiple_of(scalars[3 + at] * tokens, tokens), tokens)
        piece = pieces[min(at, 2)]
        first = (which + 2 * (at - 2 if at > 2 else 0)) * tokens
        pairs.append((piece.at[pl.ds(first, tokens), :], target.at[place, :]))
    return pairs


def ffn_body(n_parts, n_z, n_alias, scalars, *refs):
    pieces = refs[:3]
    gateup = refs[3 : 3 + n_parts]
    down = refs[3 + n_parts : 3 + 2 * n_parts]
    refs = refs[3 + 2 * n_parts + n_alias :]
    b_rows, d_rows, hid, grad_pair, keep, send, wide, deep, sems = refs
    part = down[0].shape[2]
    copies = start_copies(natural_rows(scalars, pieces, 0, b_rows), sems)
    copies += start_weights(scalars, 7, gateup, (), wide, None, sems, 4)
    later = start_copies(natural_rows(scalars, pieces, 1, d_rows), sems, len(copies))
    later += start_weights(scalars, 7, (), down, None, deep, sems, len(copies) + 4)
    for copy in copies:
        copy.wait()
    pre = dot_plain(b_rows[...], wide[...])
    for copy in later:
        copy.wait()
    d_hid = dot_plain(d_rows[...], deep[...])
    gate_pre, up_pre = pre[:, :part], pre[:, part:]
    sigma = jax.nn.sigmoid(gate_pre)
    silu = gate_pre * sigma
    hid[...] = rounded(silu * up_pre)
    d_gate = d_hid * up_pre * (sigma * (1.0 + gate_pre * (1.0 - sigma)))
    grad_pair[:, :part] = rounded(d_gate)
    grad_pair[:, part:] = rounded(d_hid * silu)
    grad_in = rounded(dot_rows(grad_pair[...], wide[...]))
    lay_out(grad_in, scalars, keep, send)


def start_weights(index, first, gateup, down, wide, deep, sems, first_sem=0):
    pairs = []
    for i, piece in enumerate(gateup):
        n_z, _, depth, part = piece.shape
        for z in range(n_z):
            block = block_rows_of(index, first + i * n_z + z, depth)
            for half in range(2):
                pairs.append((piece.at[z, half], wide.at[block, pl.ds(half * part, part)]))
    for i, piece in enumerate(down):
        n_z, depth, _ = piece.shape
        for z in range(n_z):
            pairs.append((piece.at[z], deep.at[block_rows_of(index, first + i * n_z + z, depth), :]))
    return start_copies(pairs, sems, first_sem)


def cost(flops, nbytes):
    return pl.CostEstimate(flops=flops, bytes_accessed=nbytes, transcendentals=0)


def bf16_of(*shape):
    return jax.ShapeDtypeStruct(shape, jnp.bfloat16)


def attend(index, pieces, weights, cosine, sine, bias, heads, group):
    rows, width = cosine.shape[0], pieces[0].shape[1]
    n_blocks, wide = len(weights), (heads + 4) * HD
    return pl.pallas_call(
        lambda *refs: attend_body(n_blocks, heads, group, *refs),
        out_shape=(
            bf16_of(rows, width),
            bf16_of(heads, rows, 128),
            bf16_of(2, rows, 128),
            bf16_of(rows, heads * HD),
            jax.ShapeDtypeStruct((rows, 128), jnp.float32),
        ),
        in_specs=[SMEM] + [HBM] * (3 + n_blocks) + [VMEM] * 3,
        out_specs=(VMEM,) * 5,
        scratch_shapes=[
            pltpu.VMEM((width, wide), jnp.bfloat16),
            pltpu.SemaphoreType.DMA((3 + n_blocks,)),
        ],
        cost_estimate=cost(2 * rows * width * wide + 4 * heads * rows * rows * 128, 8 << 20),
        name="attend",
    )(index, *pieces, *weights, cosine, sine, bias)


def attend_back(index, grad_rows, weights, queries, keyvals, bias, logs, cosine, sine, heads, group):
    rows, width = grad_rows.shape
    n_blocks, wide = len(weights), heads * HD
    return pl.pallas_call(
        lambda *refs: attend_back_body(n_blocks, heads, group, *refs),
        out_shape=bf16_of(rows, heads * HD + 256),
        in_specs=[SMEM, VMEM] + [HBM] * n_blocks + [VMEM] * 6,
        out_specs=VMEM,
        scratch_shapes=[
            pltpu.VMEM((width, wide), jnp.bfloat16),
            pltpu.VMEM((heads, CHUNK, 128), jnp.bfloat16),
            pltpu.VMEM((rows, 128), jnp.float32),
            pltpu.VMEM((rows, 128), jnp.float32),
            pltpu.SemaphoreType.DMA((n_blocks,)),
        ],
        cost_estimate=cost(2 * rows * width * wide + 10 * heads * rows * rows * 128, 8 << 20),
        name="attend_back",
    )(index, grad_rows, *weights, queries, keyvals, bias, logs, cosine, sine)


def rows_out(index, left, weights, first, name):
    rows, wide = left.shape
    n_blocks = len(weights)
    width = n_blocks * weights[0].shape[0]
    return pl.pallas_call(
        lambda *refs: rows_out_body(n_blocks, first, *refs),
        out_shape=(bf16_of(rows // 2, width),) * 2,
        in_specs=[SMEM, VMEM] + [HBM] * n_blocks,
        out_specs=(VMEM,) * 2,
        scratch_shapes=[
            pltpu.VMEM((width, wide), jnp.bfloat16),
            pltpu.SemaphoreType.DMA((n_blocks,)),
        ],
        cost_estimate=cost(2 * rows * width * wide, 6 << 20),
        name=name,
    )(index, left, *weights)


def ffn_rows(scalars, pieces, gateup, down, total, earlier):
    row_len, width = 2 * pieces[0].shape[0], pieces[0].shape[1]
    n_parts, n_z, part = len(gateup), gateup[0].shape[0], gateup[0].shape[3]
    n_alias = len(earlier)

    def block(wide):
        return pl.BlockSpec((row_len, wide), lambda i, scalars: (scalars[0], 0))

    def whole(wide):
        return pl.BlockSpec((row_len // 2, wide), lambda i, scalars: (0, 0))

    return pl.pallas_call(
        lambda *refs: ffn_body(n_parts, n_z, n_alias, *refs),
        grid_spec=pltpu.PrefetchScalarGridSpec(
            num_scalar_prefetch=1,
            grid=(1,),
            in_specs=[HBM] * (3 + 2 * n_parts + n_alias),
            out_specs=(block(width), block(width), block(part), block(2 * part), whole(width), whole(width)),
            scratch_shapes=[
                pltpu.VMEM((width, 2 * part), jnp.bfloat16),
                pltpu.VMEM((width, part), jnp.bfloat16),
                pltpu.SemaphoreType.DMA((8 + 3 * n_parts * n_z,)),
            ],
        ),
        out_shape=(
            bf16_of(total, width),
            bf16_of(total, width),
            bf16_of(total, part),
            bf16_of(total, 2 * part),
            bf16_of(row_len // 2, width),
            bf16_of(row_len // 2, width),
        ),
        input_output_aliases={4 + 2 * n_parts + at: at for at in range(n_alias)},
        cost_estimate=cost(row_len * width, 1 << 20),
        name="ffn_rows",
    )(scalars, *pieces, *gateup, *down, *earlier)


def lay_out(value, scalars, keep, send, lead=()):
    tokens = value.shape[0] // 4
    for place in range(4):
        piece = value[place * tokens : (place + 1) * tokens, :]
        target = pl.ds(pl.multiple_of(((place // 2) ^ scalars[1]) * tokens, tokens), tokens)

        @pl.when(scalars[2] == place % 2)
        def _():
            keep[(*lead, target, slice(None))] = piece

        @pl.when(scalars[2] != place % 2)
        def _():
            send[(*lead, target, slice(None))] = piece


def out_rows_body(n_parts, scalars, left, *refs):
    down = refs[:n_parts]
    keep, send, deep, sems = refs[n_parts:]

    @pl.when(pl.program_id(0) == 0)
    def _():
        for copy in start_weights(scalars, 7, (), down, None, deep, sems):
            copy.wait()

    lay_out(rounded(dot_rows(left[...], deep[...])), scalars, keep, send, (0,))


def out_rows(scalars, left, down, row_len):
    rows, part = left.shape
    n_parts, n_z, depth = len(down), down[0].shape[0], down[0].shape[1]
    width, n_rows = n_parts * n_z * depth, rows // row_len
    block = pl.BlockSpec((1, row_len // 2, width), lambda i, scalars: (i, 0, 0))
    return pl.pallas_call(
        lambda *refs: out_rows_body(n_parts, *refs),
        grid_spec=pltpu.PrefetchScalarGridSpec(
            num_scalar_prefetch=1,
            grid=(n_rows,),
            in_specs=[pl.BlockSpec((row_len, part), lambda i, scalars: (i, 0))] + [HBM] * n_parts,
            out_specs=(block, block),
            scratch_shapes=[
                pltpu.VMEM((width, part), jnp.bfloat16),
                pltpu.SemaphoreType.DMA((n_parts * n_z,)),
            ],
        ),
        out_shape=(bf16_of(n_rows, row_len // 2, width),) * 2,
        cost_estimate=cost(rows * width, 1 << 20),
        name="out_rows",
    )(scalars, left, *down)


def lamb_update(gradient, moment, second, weight):
    new_moment = BETA * moment + (1.0 - BETA) * gradient
    new_second = BETA * second + (1.0 - BETA) * gradient * gradient
    update = new_moment / (jnp.sqrt(new_second) + LAMB_EPS) + DECAY * weight
    return (new_moment, new_second, update)


def tile_sum(value):
    rows, wide = value.shape
    step = min(wide, 128)
    total = value[:, :step]
    for at in range(1, wide // step):
        total = total + value[:, at * step : (at + 1) * step]
    return jnp.sum(total.reshape(rows // 8, 8, step), axis=0)


def lamb_step(gradient, refs, place):
    moment, second, weight, grad_out, moment_out, second_out = refs
    new_moment, new_second, update = lamb_update(
        gradient, moment[place], second[place], weight[place]
    )
    grad_out[place] = gradient
    moment_out[place] = new_moment
    second_out[place] = new_second
    return tile_sum(update * update), tile_sum(weight[place] * weight[place])


def lamb_gateup_body(grads, *refs):
    sums = refs[6]
    update_sq, weight_sq = lamb_step(widened(grads[0]), refs[:6], 0)

    @pl.when(pl.program_id(1) == 0)
    def _():
        sums[...] = jnp.zeros_like(sums)

    sums[0, 0] += update_sq
    sums[0, 1] += weight_sq


def lamb_gateup(grads, moment, second, weight):
    two, depth, held = weight.shape
    n_z, part = grads.shape[0], held // grads.shape[0]
    block = pl.BlockSpec((1, depth, part), lambda half, z: (half, 0, z))
    whole = jax.ShapeDtypeStruct(weight.shape, jnp.float32)
    return pl.pallas_call(
        lamb_gateup_body,
        grid=(two, n_z),
        in_specs=[pl.BlockSpec((1, depth, part), lambda half, z: (z, 0, half))] + [block] * 3,
        out_specs=(block,) * 3 + (pl.BlockSpec((1, 2, 8, 128), lambda half, z: (half, 0, 0, 0)),),
        out_shape=(whole,) * 3 + (jax.ShapeDtypeStruct((two, 2, 8, 128), jnp.float32),),
        cost_estimate=cost(20 * weight.size, 26 * weight.size),
        name="lamb_gateup",
    )(grads, moment, second, weight)


def lamb_turned_body(n_sum, grads, *refs):
    sums = refs[6]
    gradient = widened(grads[0])
    for at in range(1, n_sum):
        gradient = gradient + widened(grads[at])
    update_sq, weight_sq = lamb_step(gradient.T, refs[:6], ...)

    @pl.when(pl.program_id(0) == 0)
    def _():
        sums[...] = jnp.zeros_like(sums)

    step = update_sq.shape[1]
    sums[0, :, :step] += update_sq
    sums[1, :, :step] += weight_sq


def lamb_turned(grads, moment, second, weight, n_sum, name):
    rows, depth = grads.shape[2], grads.shape[1]
    block = pl.BlockSpec((rows, depth), lambda i: (i, 0))
    whole = jax.ShapeDtypeStruct(weight.shape, jnp.float32)
    return pl.pallas_call(
        lambda *refs: lamb_turned_body(n_sum, *refs),
        grid=(weight.shape[0] // rows,),
        in_specs=[pl.BlockSpec((n_sum, depth, rows), lambda i: (i, 0, 0))] + [block] * 3,
        out_specs=(block,) * 3 + (pl.BlockSpec((2, 8, 128), lambda i: (0, 0, 0)),),
        out_shape=(whole,) * 3 + (jax.ShapeDtypeStruct((2, 8, 128), jnp.float32),),
        cost_estimate=cost(20 * weight.size, 26 * weight.size),
        name=name,
    )(grads, moment, second, weight)


def lamb_qkv_body(grads, *refs):
    query, keyval, sums = refs[0:3] + refs[6:9], refs[3:6] + refs[9:12], refs[12]
    gradient = widened(grads[0])
    for at in range(1, grads.shape[0]):
        gradient = gradient + widened(grads[at])
    wide, narrow = query[0].shape[1], keyval[0].shape[2]
    sums[0, 0], sums[0, 1] = lamb_step(gradient[:, :wide], query, ...)
    for at in range(2):
        first = wide + at * narrow
        sums[1 + at, 0], sums[1 + at, 1] = lamb_step(
            gradient[:, first : first + narrow], keyval, at
        )


def lamb_qkv(grads, query, keyval):
    shapes = [jax.ShapeDtypeStruct(part[0].shape, jnp.float32) for part in (query, keyval)]
    return pl.pallas_call(
        lamb_qkv_body,
        in_specs=[VMEM] * 7,
        out_specs=(VMEM,) * 7,
        out_shape=(shapes[0],) * 3
        + (shapes[1],) * 3
        + (jax.ShapeDtypeStruct((3, 2, 8, 128), jnp.float32),),
        cost_estimate=cost(4 << 20, 6 << 20),
        name="lamb_qkv",
    )(grads, *query, *keyval)


def lamb_moments(gradient, moment, second):
    new_moment = BETA * moment + (1.0 - BETA) * gradient
    new_second = BETA * second + (1.0 - BETA) * gradient * gradient
    return (new_moment, new_second, new_moment / (jnp.sqrt(new_second) + LAMB_EPS))


def per_device(
    hidden_in,
    out_grad,
    doc_lengths,
    norm_gains,
    w_query,
    w_keyval,
    w_out,
    w_gateup,
    w_down,
    moment_gains,
    moment_query,
    moment_keyval,
    moment_out,
    moment_gateup,
    moment_down,
    second_gains,
    second_query,
    second_keyval,
    second_out,
    second_gateup,
    second_down,
):
    tok = hidden_in.shape[1]
    width = hidden_in.shape[2]
    row_len = tok * 4
    n_o, n_z, n_x = lax.axis_size("o"), lax.axis_size("z"), lax.axis_size("x")
    n_parts = n_o * n_x
    depth = w_query.shape[0]
    heads_wide = w_query.shape[1]
    kv_wide = w_keyval.shape[2]
    local_heads = heads_wide // HD
    group_size = heads_wide // kv_wide
    ff_held = w_down.shape[0]
    ff_part = ff_held // n_z
    my_part = lax.axis_index("o") * n_x + lax.axis_index("x")
    my_z = lax.axis_index("z")

    part_of = my_part ^ jnp.arange(n_parts, dtype=jnp.int32)[:, None]
    z_of = jnp.arange(n_z, dtype=jnp.int32)[None, :]

    def block_of(part, z):
        return (((part // n_x) * n_z + z) * n_x + part % n_x).reshape(-1)

    y_at, c_at = lax.axis_index("y"), lax.axis_index("c")
    attn_index = block_of(part_of, my_z ^ z_of)
    ffn_index = block_of(part_of, z_of)

    token_block = [
        (y_at ^ y_other) * 2 + (c_at ^ c_other) for c_other in range(2) for y_other in range(2)
    ]

    def row_scalars(place):
        return jnp.concatenate([jnp.stack([my_z ^ place, y_at, c_at] + token_block), ffn_index])

    parts = range(1, n_parts)

    def to_parts(piece, what):
        return [exchange(piece, ("o", "x"), place, what) for place in parts]

    def in_order(column, across):
        return list(column) + [across[z][place - 1] for place in parts for z in range(n_z)]

    position = jnp.concatenate(
        [block * tok + jnp.arange(tok, dtype=jnp.int32) for block in token_block]
    )

    x_float = widened(hidden_in[0])
    gain_attn = norm_gains[0]
    gain_ffn = norm_gains[1]
    inv_one = lax.rsqrt(jnp.mean(x_float * x_float, axis=-1, keepdims=True) + EPS_NORM)
    normed_one = x_float * inv_one
    qkv_own = rounded(jnp.concatenate([w_query, w_keyval[0], w_keyval[1]], axis=1))
    qkv_near = exchange(qkv_own, "z", 1, "wqkv_z1")
    qkv_far = exchange(qkv_own, "z", 2, "wqkv_z2")
    qkv_x0 = to_parts(qkv_own, "wqkv_x0")
    phase_a = (qkv_near, qkv_far, *qkv_x0)
    qkv_last = exchange(after(qkv_far, *phase_a), "z", 1, "wqkv_z3")
    qkv_x1 = to_parts(after(qkv_near, *phase_a), "wqkv_x1")
    qkv_x2 = to_parts(after(qkv_far, *phase_a), "wqkv_x2")
    attn_own = after(rounded(normed_one * gain_attn), *phase_a)
    attn_across = exchange(attn_own, "y", 1, "a_y")
    phase_b = (qkv_last, *qkv_x1, *qkv_x2, attn_across)
    out_own = after(rounded(w_out.T), *phase_b)
    out_near = exchange(out_own, "z", 1, "wout_z1")
    out_far = exchange(out_own, "z", 2, "wout_z2")
    out_x0 = to_parts(out_own, "wout_x0")
    qkv_x3 = to_parts(after(qkv_last, *phase_b), "wqkv_x3")
    attn_pair = jnp.concatenate([attn_own, after(attn_across, *phase_b)])
    attn_pieces = (attn_own, attn_across, exchange(attn_pair, "c", 1, "a_c"))
    phase_c = (out_near, out_far, *out_x0, *qkv_x3)
    out_last = exchange(after(out_far, *phase_c), "z", 1, "wout_z3")
    out_x1 = to_parts(after(out_near, *phase_c), "wout_x1")
    out_x2 = to_parts(after(out_far, *phase_c), "wout_x2")
    out_x3 = to_parts(out_last, "wout_x3")
    qkv_w = in_order(
        (qkv_own, qkv_near, qkv_far, qkv_last), (qkv_x0, qkv_x1, qkv_x2, qkv_x3)
    )
    out_w = in_order(
        (out_own, out_near, out_far, out_last), (out_x0, out_x1, out_x2, out_x3)
    )
    gateup_send = rounded(w_gateup).reshape(2, depth, n_z, ff_part).transpose(2, 0, 1, 3)
    gateup_own = resplit(after(gateup_send, out_last), "wgu_z")
    segment, doc_place = doc_layout(doc_lengths[0], position)
    cosine, sine_part = rope_tables(doc_place, HD)
    cosine = jnp.concatenate([cosine] * 4, axis=1)
    sine_part = jnp.concatenate([-sine_part, sine_part] * 2, axis=1)
    bias = jnp.where(
        (segment[:, None] == segment[None, :]) & (position[None, :] <= position[:, None]),
        jnp.float32(0.0),
        jnp.float32(NEG_FILL),
    )
    attn_input, queries, keyvals, context, logs = attend(
        after(attn_index, out_last), attn_pieces, qkv_w, cosine, sine_part, bias, local_heads, group_size
    )
    mid_stream = x_float + scatter_row(
        *rows_out(attn_index, context, out_w, 0, "mid_rows"), "mid"
    )
    inv_two = lax.rsqrt(jnp.mean(mid_stream * mid_stream, axis=-1, keepdims=True) + EPS_NORM)
    normed_two = mid_stream * inv_two

    pair_own = jnp.concatenate(
        [rounded(normed_two * gain_ffn), after(out_grad[0], gateup_own)]
    )
    pair_far = exchange(pair_own, "z", 2, "bd_z2")
    pair_near = exchange(pair_own, "z", 1, "bd_z1")
    pair_rows = {0: gather_row(pair_own, "bd0")}
    down_turned = rounded(w_down).reshape(n_z, ff_part, depth).transpose(0, 2, 1)
    down_send = after(down_turned, pair_own)
    down_own = resplit(down_send, "wd_z")
    gateup_w = [gateup_own] + [
        exchange(gateup_own, ("o", "x"), place, "wgu_x") for place in range(1, n_parts)
    ]
    down_w = [down_own] + [
        exchange(after(down_own, gateup_w[-1]), ("o", "x"), place, "wd_x")
        for place in range(1, n_parts)
    ]

    pair_last = exchange(
        after(pair_far, pair_near), "z", 1, "bd_z3"
    )
    pair_rows[1] = gather_row(after(pair_near, pair_rows[0][1]), "bd1")
    held, rows = (), {}

    def ffn_row(place, *waits):
        *outs, keep, send = ffn_rows(
            after(row_scalars(place), *waits),
            pair_rows[place],
            gateup_w,
            down_w,
            n_z * row_len,
            held,
        )
        rows[place] = RowSum(keep, send, "db" + str(place))
        return tuple(outs), send

    held, sent = ffn_row(0, pair_near, pair_far)
    far_across = exchange(after(pair_far, sent), "y", 1, "bd2_y")
    held, sent1 = ffn_row(1, pair_last)
    pair_rows[2] = gather_core(pair_far, far_across, "bd2", sent1)
    last_across = exchange(after(pair_last, sent), "y", 1, "bd3_y")
    held, sent2 = ffn_row(2)
    pair_rows[3] = gather_core(pair_last, last_across, "bd3", sent2)
    for place in (1, 0, 2):
        rows[place].pass_on(last_across)
    held, sent = ffn_row(3, rows[1].received)
    rows[3].pass_on()
    ffn_input, grad_full, hidden_act, grad_pair = held

    def parts_of(weight_grad):
        cut = weight_grad.reshape(n_o, n_z, n_x, depth, weight_grad.shape[1])
        return [
            lax.dynamic_index_in_dim(
                lax.dynamic_index_in_dim(cut, (my_part ^ place) // n_x, 0, keepdims=False),
                (my_part ^ place) % n_x,
                1,
                keepdims=False,
            )
            for place in range(n_parts)
        ]

    def part_moves(pieces, what, *waits):
        return [pieces[0]] + [
            exchange(after(pieces[place], *waits), ("o", "x"), place, what + "_x")
            for place in range(1, n_parts)
        ]

    def part_sum(pieces, *waits):
        total = widened(after(pieces[0], *waits))
        for piece in pieces[1:]:
            total = total + widened(piece)
        return rounded(total)

    down_pieces = parts_of(
        rounded(dot_cols(grad_full, after(hidden_act, rows[3].received)))
    )
    gateup_pieces = parts_of(
        rounded(dot_cols(ffn_input, after(grad_pair, down_pieces[-1])))
    )
    down_moves = part_moves(down_pieces, "gdown")
    out_keep, out_send = out_rows(
        row_scalars(0), after(hidden_act, gateup_pieces[-1]), down_w, row_len
    )
    gateup_moves = part_moves(gateup_pieces, "ggu")
    near_sum = exchange(rounded(rows[1].total()), "z", 1, "db1_z")
    last_sum = exchange(after(rounded(rows[3].total()), near_sum), "z", 1, "db3_z")
    far_sum = exchange(
        after(rounded(rows[2].total() + widened(last_sum)), *down_moves[1:]), "z", 2, "db2_z"
    )
    grad_ffn_in = rows[0].total() + widened(near_sum) + widened(far_sum)
    grad_ffn_in = after(grad_ffn_in, out_send, *down_moves[1:])

    gain_grad_ffn = jnp.sum(grad_ffn_in * normed_two, axis=0)
    grad_normed_two = grad_ffn_in * gain_ffn
    grad_mid = widened(out_grad[0]) + inv_two * (
        grad_normed_two
        - normed_two * jnp.mean(grad_normed_two * normed_two, axis=-1, keepdims=True)
    )
    def ratios_of(totals):
        norms = jnp.sqrt(jnp.sum(totals.reshape(-1, 2, 1024), axis=2))
        return norms[:, 1], norms[:, 0], norms[:, 1] / norms[:, 0]

    def stepped(weight, entry, ratio):
        update = entry[1] / (jnp.sqrt(entry[2]) + LAMB_EPS) + DECAY * weight
        return weight - RATE * (update * ratio)

    grad_mid_send = rounded(grad_mid)
    grad_mid_rows = gather_row(grad_mid_send, "dmid")
    down_grads = resplit(part_sum(down_moves), "gdown_z")
    grad_mid_full = after(jnp.concatenate(grad_mid_rows), down_grads, *gateup_moves[1:])
    out_received = exchange(out_send, "c", 1, "out_c")
    out_passed = rounded(
        widened(out_keep[:, tok:]) + widened(out_received[:, tok:])
    )
    out_across = exchange(out_passed, "y", 1, "out_y")
    grad_qkv = attend_back(
        attn_index,
        after(grad_mid_full, out_passed),
        out_w,
        queries,
        keyvals,
        bias,
        logs,
        cosine,
        sine_part,
        local_heads,
        group_size,
    )
    qkv_pieces = parts_of(
        rounded(dot_cols(attn_input, grad_qkv))
    )
    qkv_moves = part_moves(qkv_pieces, "gqkv")
    out_pieces = parts_of(
        rounded(dot_cols(after(grad_mid_full, *qkv_moves), context))
    )
    out_moves = part_moves(out_pieces, "gout")
    gateup_grads = resplit(after(part_sum(gateup_moves), down_grads), "ggu_z")
    out_total = rounded(
        widened(out_keep[:, :tok]) + widened(out_received[:, :tok]) + widened(out_across)
    )
    *down_new, down_sq = lamb_turned(
        after(down_grads, qkv_pieces[-1]), moment_down, second_down, w_down, 1, "lamb_down"
    )
    ffn_out = resplit(after(out_total, gateup_grads, down_sq, qkv_pieces[-1]), "out_z")
    *gateup_new, gateup_sq = lamb_gateup(gateup_grads, moment_gateup, second_gateup, w_gateup)
    out_grads = resplit(after(part_sum(out_moves), ffn_out, gateup_sq), "gout_z")
    qkv_total = part_sum(qkv_moves)
    block_out = rounded(mid_stream + jnp.sum(widened(ffn_out), axis=0))[None]
    grad_attn_in = scatter_row(*rows_out(attn_index, grad_qkv, qkv_w, 0, "grad_rows"), "da")
    gain_grad_attn = jnp.sum(grad_attn_in * normed_one, axis=0)
    grad_normed_one = grad_attn_in * gain_attn
    input_grad = grad_mid + inv_one * (
        grad_normed_one
        - normed_one * jnp.mean(grad_normed_one * normed_one, axis=-1, keepdims=True)
    )
    gain_rows = 2 * width // 128
    packed = all_sum(
        jnp.concatenate(
            [gain_grad_attn.reshape(-1, 128), gain_grad_ffn.reshape(-1, 128)]
            + [gateup_sq.reshape(-1, 128), down_sq.reshape(-1, 128)]
        )
    )
    qkv_grads = resplit(after(qkv_total, out_grads), "gqkv_z")
    ffn_norms = ratios_of(packed[gain_rows:])
    new_gateup = stepped(w_gateup, gateup_new, ffn_norms[2][:2][:, None, None])
    new_down = stepped(w_down, down_new, ffn_norms[2][2])
    grad_gains = packed[:gain_rows].reshape(2, width)
    gain_moment, gain_second, gain_direction = lamb_moments(grad_gains, moment_gains, second_gains)
    gain_update = gain_direction + DECAY * norm_gains
    gain_norms = (
        jnp.sqrt(jnp.sum(norm_gains * norm_gains, axis=1)),
        jnp.sqrt(jnp.sum(gain_update * gain_update, axis=1)),
    )
    gain_norms = gain_norms + (gain_norms[0] / gain_norms[1],)
    new_gains = norm_gains - RATE * gain_norms[2][:, None] * gain_update

    *out_new, out_sq = lamb_turned(out_grads, moment_out, second_out, w_out, n_z, "lamb_out")
    *qkv_new, qkv_sq = lamb_qkv(
        after(qkv_grads, new_gateup, new_down, new_gains, out_sq, block_out, input_grad),
        (moment_query, second_query, w_query),
        (moment_keyval, second_keyval, w_keyval),
    )
    attn_sq = all_sum(jnp.concatenate([qkv_sq, out_sq[None]]).reshape(-1, 128))
    attn_norms = ratios_of(attn_sq)
    new_query = stepped(w_query, qkv_new[:3], attn_norms[2][0])
    new_keyval = stepped(w_keyval, qkv_new[3:], attn_norms[2][1:3][:, None, None])
    new_out = stepped(w_out, out_new, attn_norms[2][3])
    results = (qkv_new[:3], qkv_new[3:], out_new, gateup_new, down_new)
    grad_parts = tuple((entry[0] for entry in results))
    new_moments = tuple((entry[1] for entry in results))
    new_seconds = tuple((entry[2] for entry in results))
    new_parts = (new_query, new_keyval, new_out, new_gateup, new_down)
    weight_norms, update_norms, trust_ratios = (
        jnp.concatenate([attn_norms[at], ffn_norms[at], gain_norms[at]]) for at in range(3)
    )
    return (
        block_out,
        input_grad[None],
        grad_gains,
        grad_parts[0],
        grad_parts[1],
        grad_parts[2],
        grad_parts[3],
        grad_parts[4],
        new_gains,
        new_parts[0],
        new_parts[1],
        new_parts[2],
        new_parts[3],
        new_parts[4],
        gain_moment,
        new_moments[0],
        new_moments[1],
        new_moments[2],
        new_moments[3],
        new_moments[4],
        gain_second,
        new_seconds[0],
        new_seconds[1],
        new_seconds[2],
        new_seconds[3],
        new_seconds[4],
        weight_norms,
        update_norms,
        trust_ratios,
    )


def solution(mesh):
    n_dp, n_tensor = mesh.devices.shape
    split = jax.sharding.Mesh(
        mesh.devices.reshape(n_dp // 8, 4, 2, n_tensor // 2, 2), ("o", "z", "x", "y", "c")
    )
    dp, tensor = ("o", "z", "x"), ("y", "c")
    in_specs = (
        P(dp, tensor, None),
        P(dp, tensor, None),
        P(dp, None),
        P(),
        P(dp, tensor),
        P(None, dp, tensor),
        P(tensor, dp),
        P(None, dp, tensor),
        P(tensor, dp),
        P(),
        P(dp, tensor),
        P(None, dp, tensor),
        P(tensor, dp),
        P(None, dp, tensor),
        P(tensor, dp),
        P(),
        P(dp, tensor),
        P(None, dp, tensor),
        P(tensor, dp),
        P(None, dp, tensor),
        P(tensor, dp),
    )
    out_specs = (
        P(dp, tensor, None),
        P(dp, tensor, None),
        P(),
        P(dp, tensor),
        P(None, dp, tensor),
        P(tensor, dp),
        P(None, dp, tensor),
        P(tensor, dp),
        P(),
        P(dp, tensor),
        P(None, dp, tensor),
        P(tensor, dp),
        P(None, dp, tensor),
        P(tensor, dp),
        P(),
        P(dp, tensor),
        P(None, dp, tensor),
        P(tensor, dp),
        P(None, dp, tensor),
        P(tensor, dp),
        P(),
        P(dp, tensor),
        P(None, dp, tensor),
        P(tensor, dp),
        P(None, dp, tensor),
        P(tensor, dp),
        P(),
        P(),
        P(),
    )
    return jax.shard_map(
        per_device, mesh=split, in_specs=in_specs, out_specs=out_specs, check_vma=False
    )
```

```python
import jax
import jax.numpy as jnp
import numpy as np
from jax import lax
from jax.experimental import pallas as pl
from jax.experimental.pallas import tpu as pltpu
from jax.sharding import PartitionSpec as P

HD = 64


EPS_NORM = 1e-05
BETA = 0.5
LAMB_EPS = 1e-06
DECAY = 0.01
RATE = 0.5
NEG_FILL = -1e30


def rope_inverse(half_dim):
    exponent = np.arange(half_dim, dtype=np.float32) * np.float32(2.0 / (2 * half_dim))
    base_freq = np.float32(1.0) / np.power(np.float32(500000.0), exponent)
    wave_len = np.float32(2.0 * np.pi) / base_freq
    smooth = (np.float32(8192.0) / wave_len - np.float32(1.0)) / np.float32(3.0)
    middle = (np.float32(1.0) - smooth) * base_freq / np.float32(32.0) + smooth * base_freq
    scaled = np.where(
        wave_len < 2048.0,
        base_freq,
        np.where(wave_len > 8192.0, base_freq / np.float32(32.0), middle),
    )
    return scaled.astype(np.float32)


def doc_layout(lengths, position):
    doc_ends = jnp.cumsum(lengths, dtype=jnp.int32)
    starts_at = doc_ends - lengths
    segment = jnp.sum(
        (position[:, None] >= doc_ends[None, :]).astype(jnp.int32), axis=1, dtype=jnp.int32
    )
    onehot_doc = (
        segment[:, None] == jnp.arange(lengths.shape[0], dtype=jnp.int32)[None, :]
    ).astype(jnp.int32)
    doc_place = position - jnp.sum(onehot_doc * starts_at[None, :], axis=1, dtype=jnp.int32)
    return (segment, doc_place)


def rope_tables(doc_place, head_dim):
    inverse = jnp.asarray(rope_inverse(head_dim // 2))
    angles = doc_place.astype(jnp.float32)[:, None] * inverse[None, :]
    return (jnp.cos(angles), jnp.sin(angles))


def rounded(value):
    return value.astype(jnp.bfloat16)


def widened(value):
    return value.astype(jnp.float32)


def dot_plain(left_side, right_side):
    return lax.dot_general(
        left_side, right_side, (((1,), (0,)), ((), ())), preferred_element_type=jnp.float32
    )


def dot_rows(left_side, right_side):
    return lax.dot_general(
        left_side, right_side, (((1,), (1,)), ((), ())), preferred_element_type=jnp.float32
    )


def dot_cols(left_side, right_side):
    return lax.dot_general(
        left_side, right_side, (((0,), (0,)), ((), ())), preferred_element_type=jnp.float32
    )


class At:
    (
        wqkv_z1,
        wqkv_z2,
        wqkv_x0,
        wqkv_z3,
        wqkv_x1,
        wqkv_x2,
        pack,
        tables,
        cosine,
        sine,
        wout_z1,
        wout_z2,
        wout_x0,
        wqkv_x3,
        a_y,
        a_c,
        wout_z3,
        wout_x1,
        wout_x2,
        wout_x3,
        wgu_z,
        attend,
        mid_c,
        mid_add,
        mid_y,
        pair,
        bd_z2,
        bd_z1,
        wgu_x,
        wd_z,
        wd_x,
        bd_z3,
        bd0_y,
        bd0_c,
        bd1_y,
        bd1_c,
        bd2_y,
        bd2_c,
        bd3_y,
        bd3_c,
        ffn0,
        ffn1,
        ffn2,
        ffn3,
        db0_c,
        db0_add,
        db0_y,
        db1_c,
        db1_add,
        db1_y,
        db2_c,
        db2_add,
        db2_y,
        db3_c,
        db3_add,
        db3_y,
        db1_z,
        db3_z,
        db2_z,
        gdown,
        gdown_x,
        gdown_own,
        ggu,
        ggu_x,
        ggu_own,
        gqkv,
        gqkv_x,
        gqkv_own,
        gout,
        gout_x,
        gout_own,
        out_rows,
        gdown_z,
        out_c,
        out_add,
        ffnin,
        dmid_y,
        dmid_c,
        out_y,
        ggu_z,
        dmid,
        attend_back,
        lamb_down,
        grad_rows,
        da_c,
        da_add,
        da_y,
        out_z,
        lamb_gateup,
        gout_z,
        input_grad,
        gqkv_z,
        block_out,
        sums,
        new_gateup,
        new_down,
        new_gains,
        lamb_out,
        lamb_qkv,
        swap,
    ) = range(100)


GATES = {
    At.wqkv_z3: (At.wqkv_z1, At.wqkv_x0),
    At.wqkv_x1: (At.wqkv_z2, At.wqkv_x0),
    At.wqkv_x2: (At.wqkv_x0, At.wqkv_z2),
    At.a_y: (At.wqkv_z2, At.wqkv_x0),
    At.wout_z1: (At.wqkv_z3, At.wqkv_x1, At.wqkv_x2, At.a_y, At.pack, At.tables, At.cosine, At.sine),
    At.wout_z2: (At.wqkv_z3, At.wqkv_x1, At.wqkv_x2, At.a_y, At.pack, At.tables, At.cosine, At.sine),
    At.wout_x0: (At.wqkv_z3, At.wqkv_x1, At.wqkv_x2, At.a_y, At.pack, At.tables, At.cosine, At.sine),
    At.wqkv_x3: (At.wqkv_z3, At.wqkv_x1, At.wqkv_x2, At.a_y, At.pack, At.tables, At.cosine, At.sine),
    At.a_c: (At.wqkv_z3, At.wqkv_x1, At.wqkv_x2, At.a_y, At.pack, At.tables, At.cosine, At.sine),
    At.wout_z3: (At.wout_z2, At.wout_x0, At.wqkv_x3),
    At.wout_x1: (At.wout_z1, At.wout_z2, At.wout_x0, At.wqkv_x3, At.wqkv_x1),
    At.wout_x2: (At.wout_z1, At.wout_z2, At.wout_x0, At.wqkv_x3),
    At.wgu_z: (At.wout_z3, At.pack),
    At.pair: (At.wgu_z,),
    At.wd_x: (At.wgu_x,),
    At.bd_z3: (At.wout_z3,),
    At.bd1_y: (At.bd0_y,),
    At.ffn0: (At.bd_z1,),
    At.bd2_y: (At.bd_z1,),
    At.ffn1: (At.bd_z3,),
    At.bd2_c: (At.ffn1, At.wgu_x),
    At.bd3_y: (At.ffn0,),
    At.db1_add: (At.bd3_y, At.db2_c, At.ffn2, At.db0_c),
    At.db2_add: (At.bd3_y,),
    At.gdown: (At.db3_c,),
    At.ggu: (At.gdown,),
    At.gdown_own: (At.out_rows, At.db0_y),
    At.ggu_own: (At.gdown_x,),
    At.db3_z: (At.db1_z,),
    At.db2_z: (At.gdown_x,),
    At.ffnin: (At.out_rows, At.gdown_x),
    At.dmid: (At.ggu_x,),
    At.attend_back: (At.out_add,),
    At.gout: (At.gqkv_x,),
    At.out_z: (At.lamb_down, At.gqkv),
    At.gout_z: (At.out_z,),
    At.gqkv_z: (At.gout_z,),
    At.lamb_down: (At.gqkv,),
    At.gqkv_own: (At.gqkv, At.gout),
    At.gout_own: (At.gout,),
    At.lamb_qkv: (At.new_gateup, At.new_down, At.new_gains, At.lamb_out, At.block_out, At.input_grad),
    At.sums: (At.gqkv_own,),
    At.grad_rows: (At.out_c,),
    At.bd_z1: (At.wout_x0, At.pair),
    At.out_add: (At.gdown_z,),
    At.ffn2: (At.bd3_y,),
}
MADE = {}


def note(what, value):
    MADE[what] = value
    return value


def hold(what, value):
    waits = [MADE[name] for name in GATES.get(what, ()) if name in MADE]
    return after(value, *waits) if waits else value


def exchange(value, axis, mask, what=At.swap):
    names = axis if isinstance(axis, tuple) else (axis,)
    size = 1
    for name in names:
        size = size * lax.axis_size(name)
    pairs = [(place, place ^ mask) for place in range(size)]
    return note(what, lax.ppermute(hold(what, value), axis, pairs))


def resplit(value, what):
    return note(what, lax.all_to_all(hold(what, value), "z", 0, 0, tiled=True))


def after(value, *others):
    return lax.optimization_barrier((value,) + others)[0]


def gather_row(value, what):
    across = exchange(value, "y", 1, what)
    return gather_core(value, across, what)


def gather_core(value, across, what, *waits):
    pair = jnp.concatenate([value, after(across, *waits)])
    return (value, across, exchange(pair, "c", 1, what + 1))


class RowSum:
    def __init__(self, keep, send, what):
        self.keep, self.what = keep, what
        self.tokens = keep.shape[0] // 2
        self.received = exchange(send, "c", 1, what)

    def pass_on(self):
        tokens = self.tokens
        received = hold(self.what + 1, self.received)
        passed = rounded(widened(self.keep[tokens:]) + widened(received[tokens:]))
        self.across = exchange(passed, "y", 1, self.what + 2)

    def total(self):
        tokens = self.tokens
        return (
            widened(self.keep[:tokens])
            + widened(self.received[:tokens])
            + widened(self.across)
        )


def scatter_row(keep, send, what):
    row = RowSum(keep, send, what)
    row.pass_on()
    return row.total()


def all_sum(value):
    for axis in ("c", "x", "y", "z", "o"):
        mask = 1
        while mask < lax.axis_size(axis):
            value = value + exchange(value, axis, mask)
            mask = mask * 2
    return value


HBM = pl.BlockSpec(memory_space=pl.ANY)
VMEM = pl.BlockSpec(memory_space=pltpu.VMEM)
SMEM = pl.BlockSpec(memory_space=pltpu.SMEM)


def start_copies(pairs, sems, first=0):
    copies = [
        pltpu.make_async_copy(source, target, sems.at[first + place])
        for place, (source, target) in enumerate(pairs)
    ]
    for copy in copies:
        copy.start()
    return copies


def row_copies(pieces, target):
    pairs, first = [], 0
    for piece in pieces:
        pairs.append((piece, target.at[pl.ds(first, piece.shape[0]), :]))
        first += piece.shape[0]
    return pairs


def block_rows_of(index, place, depth):
    return pl.ds(pl.multiple_of(index[place] * depth, depth), depth)


def lane_iota(rows):
    return lax.broadcasted_iota(jnp.int32, (rows, 128), 1)


def partner(value):
    lane = lane_iota(value.shape[0])
    return jnp.where(lane % HD < HD // 2, pltpu.roll(value, 128 - HD // 2, 1), pltpu.roll(value, HD // 2, 1))


def head_lanes(value, head, kv):
    lane = lane_iota(value.shape[0])
    moved = value if head % 2 == kv else pltpu.roll(value, HD, 1)
    keep = lane < HD if kv == 0 else lane >= HD
    return jnp.where(keep, moved, 0.0)


def pair_slab(even, odd, kv):
    lane = lane_iota(even.shape[0])
    if kv == 0:
        odd = pltpu.roll(odd, HD, 1)
    else:
        even = pltpu.roll(even, HD, 1)
    return jnp.where(lane < HD, even, odd)


CHUNK = 256


def attend_body(n_blocks, heads, group, *refs):
    index, a_own, a_across, a_core = refs[:4]
    weights = refs[4 : 4 + n_blocks]
    cosine, sine, bias = refs[4 + n_blocks : 7 + n_blocks]
    a_all, q_out, kv_out, ctx_out, lse_out = refs[7 + n_blocks : 12 + n_blocks]
    held, sems = refs[12 + n_blocks :]
    depth = weights[0].shape[0]
    copies = start_copies(row_copies((a_own, a_across, a_core), a_all), sems)
    copies += start_copies(
        [
            (weights[i].at[:, : held.shape[1]], held.at[block_rows_of(index, i, depth), :])
            for i in range(n_blocks)
        ],
        sems,
        3,
    )
    for copy in copies:
        copy.wait()
    rows_all = a_all.shape[0]
    n_slabs = heads // 2

    @pl.loop(0, rows_all // CHUNK)
    def _(at):
        rows = pl.ds(pl.multiple_of(at * CHUNK, CHUNK), CHUNK)
        raw = dot_plain(a_all[rows, :], held[...])
        cos, sin = cosine[rows, :], sine[rows, :]
        for slab in range(n_slabs + 1):
            part = raw[:, slab * 128 : (slab + 1) * 128]
            part = part * cos + partner(part) * sin
            if slab < n_slabs:
                for head in (2 * slab, 2 * slab + 1):
                    q_out[head, rows, :] = rounded(head_lanes(part, head, head // group))
            else:
                kv_out[0, rows, :] = rounded(part)
        kv_out[1, rows, :] = rounded(raw[:, (n_slabs + 1) * 128 : (n_slabs + 2) * 128])

    @pl.loop(0, rows_all // CHUNK)
    def _(at):
        rows = pl.ds(pl.multiple_of(at * CHUNK, CHUNK), CHUNK)
        keys, values = kv_out[0], kv_out[1]
        lane = lane_iota(CHUNK)
        logs = jnp.zeros((CHUNK, 128), jnp.float32)
        for slab in range(n_slabs):
            outs = []
            for head in (2 * slab, 2 * slab + 1):
                scores = dot_rows(q_out[head, rows, :], keys) * HD ** (-0.5) + bias[rows, :]
                most = jnp.max(scores, axis=-1, keepdims=True)
                shifted = jnp.exp(scores - most)
                total = jnp.sum(shifted, axis=-1, keepdims=True)
                outs.append(dot_plain(rounded(shifted / total), values))
                logs = jnp.where(lane == head, most + jnp.log(total), logs)
            ctx_out[rows, slab * 128 : (slab + 1) * 128] = rounded(
                pair_slab(outs[0], outs[1], 2 * slab // group)
            )
        lse_out[rows, :] = logs


def attend_back_body(n_blocks, heads, group, *refs):
    index, d_all = refs[:2]
    weights = refs[2 : 2 + n_blocks]
    queries, keyvals, bias, logs, cosine, sine = refs[2 + n_blocks : 8 + n_blocks]
    out = refs[8 + n_blocks]
    held, d_heads, key_sum, value_sum, sems = refs[9 + n_blocks :]
    depth, wide = weights[0].shape[0], held.shape[1]
    first = weights[0].shape[1] - wide
    copies = start_copies(
        [
            (weights[i].at[:, pl.ds(first, wide)], held.at[block_rows_of(index, i, depth), :])
            for i in range(n_blocks)
        ],
        sems,
    )
    for copy in copies:
        copy.wait()
    rows_all = d_all.shape[0]
    n_slabs = heads // 2
    key_sum[...] = jnp.zeros_like(key_sum)
    value_sum[...] = jnp.zeros_like(value_sum)

    @pl.loop(0, rows_all // CHUNK)
    def _(at):
        rows = pl.ds(pl.multiple_of(at * CHUNK, CHUNK), CHUNK)
        d_ctx = dot_plain(d_all[rows, :], held[...])
        for slab in range(n_slabs):
            part = d_ctx[:, slab * 128 : (slab + 1) * 128]
            for head in (2 * slab, 2 * slab + 1):
                d_heads[head, :, :] = rounded(head_lanes(part, head, head // group))
        keys, values = keyvals[0], keyvals[1]
        lane = lane_iota(CHUNK)
        cos, sin = cosine[rows, :], sine[rows, :]
        log_rows = logs[rows, :]
        for slab in range(n_slabs):
            kv = 2 * slab // group
            outs = []
            for head in (2 * slab, 2 * slab + 1):
                query, d_head = queries[head, rows, :], d_heads[head]
                log_total = jnp.sum(jnp.where(lane == head, log_rows, 0.0), axis=-1, keepdims=True)
                scores = dot_rows(query, keys) * HD ** (-0.5) + bias[rows, :]
                probs = jnp.exp(scores - log_total)
                d_probs = dot_rows(d_head, values)
                inner = jnp.sum(probs * d_probs, axis=-1, keepdims=True)
                d_scores = rounded(probs * (d_probs - inner) * HD ** (-0.5))
                key_sum[...] += dot_cols(d_scores, query)
                value_sum[...] += dot_cols(rounded(probs), d_head)
                outs.append(dot_plain(d_scores, keys))
            part = pair_slab(outs[0], outs[1], kv)
            out[rows, slab * 128 : (slab + 1) * 128] = rounded(part * cos - partner(part) * sin)

    key_grad = key_sum[...]
    key_grad = key_grad * cosine[...] - partner(key_grad) * sine[...]
    out[:, n_slabs * 128 : (n_slabs + 1) * 128] = rounded(key_grad)
    out[:, (n_slabs + 1) * 128 : (n_slabs + 2) * 128] = rounded(value_sum[...])


def rows_out_body(n_blocks, first, *refs):
    index, left = refs[:2]
    weights = refs[2 : 2 + n_blocks]
    keep, send, held, sems = refs[2 + n_blocks :]
    depth, wide = weights[0].shape[0], held.shape[1]
    copies = start_copies(
        [
            (weights[i].at[:, pl.ds(first, wide)], held.at[block_rows_of(index, i, depth), :])
            for i in range(n_blocks)
        ],
        sems,
    )
    for copy in copies:
        copy.wait()
    half = left.shape[0] // 2
    send[...] = rounded(dot_rows(left[half:, :], held[...]))
    keep[...] = rounded(dot_rows(left[:half, :], held[...]))


def natural_rows(scalars, pieces, which, target):
    tokens = pieces[0].shape[0] // 2
    pairs = []
    for at in range(4):
        place = pl.ds(pl.multiple_of(scalars[3 + at] * tokens, tokens), tokens)
        piece = pieces[min(at, 2)]
        first = (which + 2 * (at - 2 if at > 2 else 0)) * tokens
        pairs.append((piece.at[pl.ds(first, tokens), :], target.at[place, :]))
    return pairs


def ffn_body(n_parts, n_z, n_alias, scalars, *refs):
    pieces = refs[:3]
    gateup = refs[3 : 3 + n_parts]
    down = refs[3 + n_parts : 3 + 2 * n_parts]
    refs = refs[3 + 2 * n_parts + n_alias :]
    b_all, d_all, hid, grad_pair, keep, send, b_rows, d_rows, wide, deep, sems = refs
    first = pl.multiple_of(scalars[0] * b_rows.shape[0], b_rows.shape[0])
    own_rows = pl.ds(first, b_rows.shape[0])
    last = sems.shape[0] - 2
    part = down[0].shape[2]
    copies = start_copies(natural_rows(scalars, pieces, 0, b_rows), sems)
    copies += start_weights(scalars, 7, gateup, (), wide, None, sems, 4)
    later = start_copies(natural_rows(scalars, pieces, 1, d_rows), sems, len(copies))
    later += start_weights(scalars, 7, (), down, None, deep, sems, len(copies) + 4)
    for copy in copies:
        copy.wait()
    kept = start_copies([(b_rows, b_all.at[own_rows, :])], sems, last)
    pre = dot_plain(b_rows[...], wide[...])
    for copy in later:
        copy.wait()
    kept += start_copies([(d_rows, d_all.at[own_rows, :])], sems, last + 1)
    d_hid = dot_plain(d_rows[...], deep[...])
    gate_pre, up_pre = pre[:, :part], pre[:, part:]
    sigma = jax.nn.sigmoid(gate_pre)
    silu = gate_pre * sigma
    hid[...] = rounded(silu * up_pre)
    d_gate = d_hid * up_pre * (sigma * (1.0 + gate_pre * (1.0 - sigma)))
    grad_pair[:, :part] = rounded(d_gate)
    grad_pair[:, part:] = rounded(d_hid * silu)
    grad_in = rounded(dot_rows(grad_pair[...], wide[...]))
    lay_out(grad_in, scalars, keep, send)
    for copy in kept:
        copy.wait()


def start_weights(index, first, gateup, down, wide, deep, sems, first_sem=0):
    pairs = []
    for i, piece in enumerate(gateup):
        n_z, _, depth, part = piece.shape
        for z in range(n_z):
            block = block_rows_of(index, first + i * n_z + z, depth)
            for half in range(2):
                pairs.append((piece.at[z, half], wide.at[block, pl.ds(half * part, part)]))
    for i, piece in enumerate(down):
        n_z, depth, _ = piece.shape
        for z in range(n_z):
            pairs.append((piece.at[z], deep.at[block_rows_of(index, first + i * n_z + z, depth), :]))
    return start_copies(pairs, sems, first_sem)


def cost(flops, nbytes):
    return pl.CostEstimate(flops=flops, bytes_accessed=nbytes, transcendentals=0)


def bf16_of(*shape):
    return jax.ShapeDtypeStruct(shape, jnp.bfloat16)


def attend(index, pieces, weights, cosine, sine, bias, heads, group):
    rows, width = cosine.shape[0], pieces[0].shape[1]
    n_blocks, wide = len(weights), (heads + 4) * HD
    return pl.pallas_call(
        lambda *refs: attend_body(n_blocks, heads, group, *refs),
        out_shape=(
            bf16_of(rows, width),
            bf16_of(heads, rows, 128),
            bf16_of(2, rows, 128),
            bf16_of(rows, heads * HD),
            jax.ShapeDtypeStruct((rows, 128), jnp.float32),
        ),
        in_specs=[SMEM] + [HBM] * (3 + n_blocks) + [VMEM] * 3,
        out_specs=(VMEM,) * 5,
        scratch_shapes=[
            pltpu.VMEM((width, wide), jnp.bfloat16),
            pltpu.SemaphoreType.DMA((3 + n_blocks,)),
        ],
        cost_estimate=cost(2 * rows * width * wide + 4 * heads * rows * rows * 128, 8 << 20),
        name="attend",
    )(index, *pieces, *weights, cosine, sine, bias)


def attend_back(index, grad_rows, weights, queries, keyvals, bias, logs, cosine, sine, heads, group):
    rows, width = grad_rows.shape
    n_blocks, wide = len(weights), heads * HD
    return pl.pallas_call(
        lambda *refs: attend_back_body(n_blocks, heads, group, *refs),
        out_shape=bf16_of(rows, heads * HD + 256),
        in_specs=[SMEM, VMEM] + [HBM] * n_blocks + [VMEM] * 6,
        out_specs=VMEM,
        scratch_shapes=[
            pltpu.VMEM((width, wide), jnp.bfloat16),
            pltpu.VMEM((heads, CHUNK, 128), jnp.bfloat16),
            pltpu.VMEM((rows, 128), jnp.float32),
            pltpu.VMEM((rows, 128), jnp.float32),
            pltpu.SemaphoreType.DMA((n_blocks,)),
        ],
        cost_estimate=cost(2 * rows * width * wide + 10 * heads * rows * rows * 128, 8 << 20),
        name="attend_back",
    )(index, grad_rows, *weights, queries, keyvals, bias, logs, cosine, sine)


def rows_out(index, left, weights, first, name):
    rows, wide = left.shape
    n_blocks = len(weights)
    width = n_blocks * weights[0].shape[0]
    return pl.pallas_call(
        lambda *refs: rows_out_body(n_blocks, first, *refs),
        out_shape=(bf16_of(rows // 2, width),) * 2,
        in_specs=[SMEM, VMEM] + [HBM] * n_blocks,
        out_specs=(VMEM,) * 2,
        scratch_shapes=[
            pltpu.VMEM((width, wide), jnp.bfloat16),
            pltpu.SemaphoreType.DMA((n_blocks,)),
        ],
        cost_estimate=cost(2 * rows * width * wide, 6 << 20),
        name=name,
    )(index, left, *weights)


def ffn_rows(scalars, pieces, gateup, down, total, earlier):
    row_len, width = 2 * pieces[0].shape[0], pieces[0].shape[1]
    n_parts, n_z, part = len(gateup), gateup[0].shape[0], gateup[0].shape[3]
    n_alias = len(earlier)

    def block(wide):
        return pl.BlockSpec((row_len, wide), lambda i, scalars: (scalars[0], 0))

    def whole(wide):
        return pl.BlockSpec((row_len // 2, wide), lambda i, scalars: (0, 0))

    return pl.pallas_call(
        lambda *refs: ffn_body(n_parts, n_z, n_alias, *refs),
        grid_spec=pltpu.PrefetchScalarGridSpec(
            num_scalar_prefetch=1,
            grid=(1,),
            in_specs=[HBM] * (3 + 2 * n_parts + n_alias),
            out_specs=(HBM, HBM, block(part), block(2 * part), whole(width), whole(width)),
            scratch_shapes=[
                pltpu.VMEM((row_len, width), jnp.bfloat16),
                pltpu.VMEM((row_len, width), jnp.bfloat16),
                pltpu.VMEM((width, 2 * part), jnp.bfloat16),
                pltpu.VMEM((width, part), jnp.bfloat16),
                pltpu.SemaphoreType.DMA((10 + 3 * n_parts * n_z,)),
            ],
        ),
        out_shape=(
            bf16_of(total, width),
            bf16_of(total, width),
            bf16_of(total, part),
            bf16_of(total, 2 * part),
            bf16_of(row_len // 2, width),
            bf16_of(row_len // 2, width),
        ),
        input_output_aliases={4 + 2 * n_parts + at: at for at in range(n_alias)},
        cost_estimate=cost(row_len * width, 1 << 20),
        name="ffn_rows",
    )(scalars, *pieces, *gateup, *down, *earlier)


def weight_grad_body(index, left, right, out):
    out[0] = rounded(dot_cols(left[...], right[...]))


def weight_grad(index, part, left, right, depth, count):
    rows, wide = right.shape
    if depth % 128:
        blocks = rounded(dot_cols(left, right)).reshape(-1, depth, wide)
        return blocks[index[part * count : (part + 1) * count]]
    return pl.pallas_call(
        weight_grad_body,
        grid_spec=pltpu.PrefetchScalarGridSpec(
            num_scalar_prefetch=1,
            grid=(count,),
            in_specs=[
                pl.BlockSpec((rows, depth), lambda i, index: (0, index[part * count + i])),
                pl.BlockSpec((rows, wide), lambda i, index: (0, 0)),
            ],
            out_specs=pl.BlockSpec((1, depth, wide), lambda i, index: (i, 0, 0)),
        ),
        out_shape=bf16_of(count, depth, wide),
        cost_estimate=cost(rows * wide, 1 << 20),
        name="weight_grad",
    )(index, left, right)


def lay_out(value, scalars, keep, send, lead=()):
    tokens = value.shape[0] // 4
    for place in range(4):
        piece = value[place * tokens : (place + 1) * tokens, :]
        target = pl.ds(pl.multiple_of(((place // 2) ^ scalars[1]) * tokens, tokens), tokens)

        @pl.when(scalars[2] == place % 2)
        def _():
            keep[(*lead, target, slice(None))] = piece

        @pl.when(scalars[2] != place % 2)
        def _():
            send[(*lead, target, slice(None))] = piece


def out_rows_body(n_parts, scalars, left, *refs):
    down = refs[:n_parts]
    keep, send, deep, sems = refs[n_parts:]

    @pl.when(pl.program_id(0) == 0)
    def _():
        for copy in start_weights(scalars, 7, (), down, None, deep, sems):
            copy.wait()

    lay_out(rounded(dot_rows(left[...], deep[...])), scalars, keep, send, (0,))


def out_rows(scalars, left, down, row_len):
    rows, part = left.shape
    n_parts, n_z, depth = len(down), down[0].shape[0], down[0].shape[1]
    width, n_rows = n_parts * n_z * depth, rows // row_len
    block = pl.BlockSpec((1, row_len // 2, width), lambda i, scalars: (i, 0, 0))
    return pl.pallas_call(
        lambda *refs: out_rows_body(n_parts, *refs),
        grid_spec=pltpu.PrefetchScalarGridSpec(
            num_scalar_prefetch=1,
            grid=(n_rows,),
            in_specs=[pl.BlockSpec((row_len, part), lambda i, scalars: (i, 0))] + [HBM] * n_parts,
            out_specs=(block, block),
            scratch_shapes=[
                pltpu.VMEM((width, part), jnp.bfloat16),
                pltpu.SemaphoreType.DMA((n_parts * n_z,)),
            ],
        ),
        out_shape=(bf16_of(n_rows, row_len // 2, width),) * 2,
        cost_estimate=cost(rows * width, 1 << 20),
        name="out_rows",
    )(scalars, left, *down)


def lamb_update(gradient, moment, second, weight):
    new_moment = BETA * moment + (1.0 - BETA) * gradient
    new_second = BETA * second + (1.0 - BETA) * gradient * gradient
    update = new_moment / (jnp.sqrt(new_second) + LAMB_EPS) + DECAY * weight
    return (new_moment, new_second, update)


def tile_sum(value):
    rows, wide = value.shape
    step = min(wide, 128)
    total = value[:, :step]
    for at in range(1, wide // step):
        total = total + value[:, at * step : (at + 1) * step]
    return jnp.sum(total.reshape(rows // 8, 8, step), axis=0)


def lamb_step(gradient, refs, place):
    moment, second, weight, grad_out, moment_out, second_out = refs
    new_moment, new_second, update = lamb_update(
        gradient, moment[place], second[place], weight[place]
    )
    grad_out[place] = gradient
    moment_out[place] = new_moment
    second_out[place] = new_second
    return tile_sum(update * update), tile_sum(weight[place] * weight[place])


def lamb_gateup_body(grads, *refs):
    sums = refs[6]
    update_sq, weight_sq = lamb_step(widened(grads[0]), refs[:6], 0)

    @pl.when(pl.program_id(1) == 0)
    def _():
        sums[...] = jnp.zeros_like(sums)

    sums[0, 0] += update_sq
    sums[0, 1] += weight_sq


def lamb_gateup(grads, moment, second, weight):
    two, depth, held = weight.shape
    n_z, part = grads.shape[0], held // grads.shape[0]
    block = pl.BlockSpec((1, depth, part), lambda half, z: (half, 0, z))
    whole = jax.ShapeDtypeStruct(weight.shape, jnp.float32)
    return pl.pallas_call(
        lamb_gateup_body,
        grid=(two, n_z),
        in_specs=[pl.BlockSpec((1, depth, part), lambda half, z: (z, 0, half))] + [block] * 3,
        out_specs=(block,) * 3 + (pl.BlockSpec((1, 2, 8, 128), lambda half, z: (half, 0, 0, 0)),),
        out_shape=(whole,) * 3 + (jax.ShapeDtypeStruct((two, 2, 8, 128), jnp.float32),),
        cost_estimate=cost(20 * weight.size, 26 * weight.size),
        name="lamb_gateup",
    )(grads, moment, second, weight)


def lamb_turned_body(n_sum, grads, *refs):
    sums = refs[6]
    gradient = widened(grads[0])
    for at in range(1, n_sum):
        gradient = gradient + widened(grads[at])
    update_sq, weight_sq = lamb_step(gradient.T, refs[:6], ...)

    @pl.when(pl.program_id(0) == 0)
    def _():
        sums[...] = jnp.zeros_like(sums)

    step = update_sq.shape[1]
    sums[0, :, :step] += update_sq
    sums[1, :, :step] += weight_sq


def lamb_turned(grads, moment, second, weight, n_sum, name):
    rows, depth = grads.shape[2], grads.shape[1]
    block = pl.BlockSpec((rows, depth), lambda i: (i, 0))
    whole = jax.ShapeDtypeStruct(weight.shape, jnp.float32)
    return pl.pallas_call(
        lambda *refs: lamb_turned_body(n_sum, *refs),
        grid=(weight.shape[0] // rows,),
        in_specs=[pl.BlockSpec((n_sum, depth, rows), lambda i: (i, 0, 0))] + [block] * 3,
        out_specs=(block,) * 3 + (pl.BlockSpec((2, 8, 128), lambda i: (0, 0, 0)),),
        out_shape=(whole,) * 3 + (jax.ShapeDtypeStruct((2, 8, 128), jnp.float32),),
        cost_estimate=cost(20 * weight.size, 26 * weight.size),
        name=name,
    )(grads, moment, second, weight)


def lamb_qkv_body(grads, *refs):
    query, keyval, sums = refs[0:3] + refs[6:9], refs[3:6] + refs[9:12], refs[12]
    gradient = widened(grads[0])
    for at in range(1, grads.shape[0]):
        gradient = gradient + widened(grads[at])
    wide, narrow = query[0].shape[1], keyval[0].shape[2]
    sums[0, 0], sums[0, 1] = lamb_step(gradient[:, :wide], query, ...)
    for at in range(2):
        first = wide + at * narrow
        sums[1 + at, 0], sums[1 + at, 1] = lamb_step(
            gradient[:, first : first + narrow], keyval, at
        )


def lamb_qkv(grads, query, keyval):
    shapes = [jax.ShapeDtypeStruct(part[0].shape, jnp.float32) for part in (query, keyval)]
    return pl.pallas_call(
        lamb_qkv_body,
        in_specs=[VMEM] * 7,
        out_specs=(VMEM,) * 7,
        out_shape=(shapes[0],) * 3
        + (shapes[1],) * 3
        + (jax.ShapeDtypeStruct((3, 2, 8, 128), jnp.float32),),
        cost_estimate=cost(4 << 20, 6 << 20),
        name="lamb_qkv",
    )(grads, *query, *keyval)


def lamb_moments(gradient, moment, second):
    new_moment = BETA * moment + (1.0 - BETA) * gradient
    new_second = BETA * second + (1.0 - BETA) * gradient * gradient
    return (new_moment, new_second, new_moment / (jnp.sqrt(new_second) + LAMB_EPS))


def attn_step_body(sums, *refs):
    query, keyval, out = refs[0:3] + (refs[9],), refs[3:6] + (refs[10],), refs[6:9] + (refs[11],)
    norms = refs[12]
    lane = lane_iota(8)
    row = lax.broadcasted_iota(jnp.int32, (8, 128), 0)
    kept = jnp.zeros((8, 128), jnp.float32)
    targets = ((query, ...), (keyval, 0), (keyval, 1), (out, ...))
    for at, ((weight, moment, second, new), place) in enumerate(targets):
        update_norm, weight_norm = (
            jnp.sqrt(jnp.sum(jnp.sum(sums[at, which], axis=0, keepdims=True), axis=1, keepdims=True))
            for which in range(2)
        )
        ratio = weight_norm / update_norm
        for which, value in enumerate((weight_norm, update_norm, ratio)):
            kept = jnp.where((row == which) & (lane == at), value, kept)
        update = moment[place] / (jnp.sqrt(second[place]) + LAMB_EPS) + DECAY * weight[place]
        new[place] = weight[place] - RATE * (update * ratio)
    norms[...] = kept


def attn_step(sums, query, keyval, out):
    shapes = [jax.ShapeDtypeStruct(part[0].shape, jnp.float32) for part in (query, keyval, out)]
    return pl.pallas_call(
        attn_step_body,
        in_specs=[VMEM] * 10,
        out_specs=(VMEM,) * 4,
        out_shape=(*shapes, jax.ShapeDtypeStruct((8, 128), jnp.float32)),
        cost_estimate=cost(4 << 20, 6 << 20),
        name="attn_step",
    )(sums, *query, *keyval, *out)


def per_device(
    hidden_in,
    out_grad,
    doc_lengths,
    norm_gains,
    w_query,
    w_keyval,
    w_out,
    w_gateup,
    w_down,
    moment_gains,
    moment_query,
    moment_keyval,
    moment_out,
    moment_gateup,
    moment_down,
    second_gains,
    second_query,
    second_keyval,
    second_out,
    second_gateup,
    second_down,
):
    MADE.clear()
    tok = hidden_in.shape[1]
    width = hidden_in.shape[2]
    row_len = tok * 4
    n_o, n_z, n_x = lax.axis_size("o"), lax.axis_size("z"), lax.axis_size("x")
    n_parts = n_o * n_x
    depth = w_query.shape[0]
    heads_wide = w_query.shape[1]
    kv_wide = w_keyval.shape[2]
    local_heads = heads_wide // HD
    group_size = heads_wide // kv_wide
    ff_held = w_down.shape[0]
    ff_part = ff_held // n_z
    my_part = lax.axis_index("o") * n_x + lax.axis_index("x")
    my_z = lax.axis_index("z")

    part_of = my_part ^ jnp.arange(n_parts, dtype=jnp.int32)[:, None]
    z_of = jnp.arange(n_z, dtype=jnp.int32)[None, :]

    def block_of(part, z):
        return (((part // n_x) * n_z + z) * n_x + part % n_x).reshape(-1)

    y_at, c_at = lax.axis_index("y"), lax.axis_index("c")
    attn_index = block_of(part_of, my_z ^ z_of)
    ffn_index = block_of(part_of, z_of)

    token_block = [
        (y_at ^ y_other) * 2 + (c_at ^ c_other) for c_other in range(2) for y_other in range(2)
    ]

    def row_scalars(place):
        return jnp.concatenate([jnp.stack([my_z ^ place, y_at, c_at] + token_block), ffn_index])

    parts = range(1, n_parts)

    def to_parts(piece, what):
        return [exchange(piece, ("o", "x"), place, what) for place in parts]

    def in_order(column, across):
        return list(column) + [across[z][place - 1] for place in parts for z in range(n_z)]

    position = jnp.concatenate(
        [block * tok + jnp.arange(tok, dtype=jnp.int32) for block in token_block]
    )

    x_float = widened(hidden_in[0])
    gain_attn = norm_gains[0]
    gain_ffn = norm_gains[1]
    inv_one = lax.rsqrt(jnp.mean(x_float * x_float, axis=-1, keepdims=True) + EPS_NORM)
    normed_one = x_float * inv_one
    qkv_own = rounded(jnp.concatenate([w_query, w_keyval[0], w_keyval[1]], axis=1))
    qkv_near = exchange(qkv_own, "z", 1, At.wqkv_z1)
    qkv_far = exchange(qkv_own, "z", 2, At.wqkv_z2)
    qkv_x0 = to_parts(qkv_own, At.wqkv_x0)
    qkv_last = exchange(qkv_far, "z", 1, At.wqkv_z3)
    qkv_x1 = to_parts(qkv_near, At.wqkv_x1)
    qkv_x2 = to_parts(qkv_far, At.wqkv_x2)
    attn_own = rounded(normed_one * gain_attn)
    attn_across = exchange(attn_own, "y", 1, At.a_y)
    gateup_send = rounded(w_gateup).reshape(2, depth, n_z, ff_part).transpose(2, 0, 1, 3)
    note(At.pack, gateup_send)
    segment, doc_place = doc_layout(doc_lengths[0], position)
    cosine, sine_part = rope_tables(doc_place, HD)
    cosine = jnp.concatenate([cosine] * 4, axis=1)
    sine_part = jnp.concatenate([-sine_part, sine_part] * 2, axis=1)
    bias = jnp.where(
        (segment[:, None] == segment[None, :]) & (position[None, :] <= position[:, None]),
        jnp.float32(0.0),
        jnp.float32(NEG_FILL),
    )
    note(At.tables, bias)
    note(At.cosine, cosine)
    note(At.sine, sine_part)
    out_own = rounded(w_out.T)
    out_near = exchange(out_own, "z", 1, At.wout_z1)
    out_far = exchange(out_own, "z", 2, At.wout_z2)
    out_x0 = to_parts(out_own, At.wout_x0)
    qkv_x3 = to_parts(qkv_last, At.wqkv_x3)
    attn_pieces = gather_core(attn_own, attn_across, At.a_y)
    out_last = exchange(out_far, "z", 1, At.wout_z3)
    out_x1 = to_parts(out_near, At.wout_x1)
    out_x2 = to_parts(out_far, At.wout_x2)
    out_x3 = to_parts(out_last, At.wout_x3)
    qkv_w = in_order(
        (qkv_own, qkv_near, qkv_far, qkv_last), (qkv_x0, qkv_x1, qkv_x2, qkv_x3)
    )
    out_w = in_order(
        (out_own, out_near, out_far, out_last), (out_x0, out_x1, out_x2, out_x3)
    )
    gateup_own = resplit(gateup_send, At.wgu_z)
    attn_input, queries, keyvals, context, logs = attend(
        hold(At.attend, attn_index), attn_pieces, qkv_w, cosine, sine_part, bias, local_heads, group_size
    )
    mid_stream = x_float + scatter_row(
        *rows_out(attn_index, context, out_w, 0, "mid_rows"), At.mid_c
    )
    inv_two = lax.rsqrt(jnp.mean(mid_stream * mid_stream, axis=-1, keepdims=True) + EPS_NORM)
    normed_two = mid_stream * inv_two

    pair_own = jnp.concatenate(
        [rounded(normed_two * gain_ffn), hold(At.pair, out_grad[0])]
    )
    note(At.pair, pair_own)
    pair_far = exchange(pair_own, "z", 2, At.bd_z2)
    pair_near = exchange(pair_own, "z", 1, At.bd_z1)
    pair_across = exchange(pair_own, "y", 1, At.bd0_y)
    gateup_w = [gateup_own] + to_parts(gateup_own, At.wgu_x)
    down_turned = rounded(w_down).reshape(n_z, ff_part, depth).transpose(0, 2, 1)
    down_own = resplit(down_turned, At.wd_z)
    down_w = [down_own] + to_parts(down_own, At.wd_x)
    pair_last = exchange(pair_far, "z", 1, At.bd_z3)
    near_across = exchange(pair_near, "y", 1, At.bd1_y)
    pair_rows = {0: gather_core(pair_own, pair_across, At.bd0_y)}
    pair_rows[1] = gather_core(pair_near, near_across, At.bd1_y)
    held, rows = (), {}

    def ffn_row(place):
        *outs, keep, send = ffn_rows(
            hold(At.ffn0 + place, row_scalars(place)),
            pair_rows[place],
            gateup_w,
            down_w,
            n_z * row_len,
            held,
        )
        note(At.ffn0 + place, send)
        rows[place] = RowSum(keep, send, At.db0_c + 3 * place)
        return tuple(outs)

    held = ffn_row(0)
    far_across = exchange(pair_far, "y", 1, At.bd2_y)
    held = ffn_row(1)
    pair_rows[2] = gather_core(pair_far, far_across, At.bd2_y)
    last_across = exchange(pair_last, "y", 1, At.bd3_y)
    held = ffn_row(2)
    pair_rows[3] = gather_core(pair_last, last_across, At.bd3_y)
    for place in (1, 0, 2):
        rows[place].pass_on()
    held = ffn_row(3)
    rows[3].pass_on()
    ffn_input, grad_full, hidden_act, grad_pair = held

    def others(left, right, what):
        index = hold(what, ffn_index)
        made = [weight_grad(index, place, left, right, depth, n_z) for place in parts]
        note(what, made[-1])
        return [
            exchange(piece, ("o", "x"), place, what + 1) for place, piece in zip(parts, made)
        ]

    def with_own(left, right, moved, what):
        index = hold(what + 2, ffn_index)
        own = note(what + 2, weight_grad(index, 0, left, right, depth, n_z))
        total = widened(own)
        for piece in moved:
            total = total + widened(piece)
        return rounded(total)

    near_sum = exchange(rounded(rows[1].total()), "z", 1, At.db1_z)
    down_moves = others(grad_full, hidden_act, At.gdown)
    gateup_moves = others(ffn_input, grad_pair, At.ggu)
    last_sum = exchange(rounded(rows[3].total()), "z", 1, At.db3_z)
    far_sum = exchange(rounded(rows[2].total() + widened(last_sum)), "z", 2, At.db2_z)
    out_keep, out_send = out_rows(
        hold(At.out_rows, row_scalars(0)), hidden_act, down_w, row_len
    )
    note(At.out_rows, out_send)
    down_total = with_own(grad_full, hidden_act, down_moves, At.gdown)
    down_grads = resplit(down_total, At.gdown_z)
    out_received = exchange(out_send, "c", 1, At.out_c)
    out_passed = rounded(
        widened(out_keep[:, tok:]) + widened(hold(At.out_add, out_received)[:, tok:])
    )
    note(At.out_add, out_passed)
    grad_ffn_in = rows[0].total() + widened(near_sum) + widened(far_sum)
    grad_ffn_in = hold(At.ffnin, grad_ffn_in)

    gain_grad_ffn = jnp.sum(grad_ffn_in * normed_two, axis=0)
    grad_normed_two = grad_ffn_in * gain_ffn
    grad_mid = widened(out_grad[0]) + inv_two * (
        grad_normed_two
        - normed_two * jnp.mean(grad_normed_two * normed_two, axis=-1, keepdims=True)
    )
    grad_mid_rows = gather_row(rounded(grad_mid), At.dmid_y)
    out_across = exchange(out_passed, "y", 1, At.out_y)
    gateup_total = with_own(ffn_input, grad_pair, gateup_moves, At.ggu)
    gateup_grads = resplit(gateup_total, At.ggu_z)
    grad_mid_full = hold(At.dmid, jnp.concatenate(grad_mid_rows))
    grad_qkv = attend_back(
        hold(At.attend_back, attn_index),
        grad_mid_full,
        out_w,
        queries,
        keyvals,
        bias,
        logs,
        cosine,
        sine_part,
        local_heads,
        group_size,
    )
    note(At.attend_back, grad_qkv)
    qkv_moves = others(attn_input, grad_qkv, At.gqkv)
    out_moves = others(grad_mid_full, context, At.gout)
    *down_new, down_sq = lamb_turned(
        hold(At.lamb_down, down_grads), moment_down, second_down, w_down, 1, "lamb_down"
    )
    note(At.lamb_down, down_sq)
    grad_parts_send = rows_out(
        hold(At.grad_rows, attn_index), grad_qkv, qkv_w, 0, "grad_rows"
    )
    note(At.grad_rows, grad_parts_send[1])
    grad_attn_in = scatter_row(*grad_parts_send, At.da_c)
    out_total = rounded(
        widened(out_keep[:, :tok]) + widened(out_received[:, :tok]) + widened(out_across)
    )
    ffn_out = resplit(out_total, At.out_z)
    *gateup_new, gateup_sq = lamb_gateup(
        hold(At.lamb_gateup, gateup_grads), moment_gateup, second_gateup, w_gateup
    )
    note(At.lamb_gateup, gateup_sq)
    wout_total = with_own(grad_mid_full, context, out_moves, At.gout)
    qkv_total = with_own(attn_input, grad_qkv, qkv_moves, At.gqkv)
    out_grads = resplit(wout_total, At.gout_z)
    gain_grad_attn = jnp.sum(grad_attn_in * normed_one, axis=0)
    grad_normed_one = grad_attn_in * gain_attn
    input_grad = grad_mid + inv_one * (
        grad_normed_one
        - normed_one * jnp.mean(grad_normed_one * normed_one, axis=-1, keepdims=True)
    )
    note(At.input_grad, input_grad)
    qkv_grads = resplit(qkv_total, At.gqkv_z)
    block_out = rounded(mid_stream + jnp.sum(widened(ffn_out), axis=0))[None]
    note(At.block_out, block_out)
    gain_rows = 2 * width // 128
    packed = all_sum(
        hold(
            At.sums,
            jnp.concatenate(
                [gain_grad_attn.reshape(-1, 128), gain_grad_ffn.reshape(-1, 128)]
                + [gateup_sq.reshape(-1, 128), down_sq.reshape(-1, 128)]
            ),
        )
    )
    note(At.sums, packed)

    def ratios_of(totals):
        norms = jnp.sqrt(jnp.sum(totals.reshape(-1, 2, 1024), axis=2))
        return norms[:, 1], norms[:, 0], norms[:, 1] / norms[:, 0]

    def stepped(weight, entry, ratio):
        update = entry[1] / (jnp.sqrt(entry[2]) + LAMB_EPS) + DECAY * weight
        return weight - RATE * (update * ratio)

    ffn_norms = ratios_of(packed[gain_rows:])
    new_gateup = stepped(w_gateup, gateup_new, ffn_norms[2][:2][:, None, None])
    new_down = stepped(w_down, down_new, ffn_norms[2][2])
    grad_gains = packed[:gain_rows].reshape(2, width)
    gain_moment, gain_second, gain_direction = lamb_moments(grad_gains, moment_gains, second_gains)
    gain_update = gain_direction + DECAY * norm_gains
    gain_norms = (
        jnp.sqrt(jnp.sum(norm_gains * norm_gains, axis=1)),
        jnp.sqrt(jnp.sum(gain_update * gain_update, axis=1)),
    )
    gain_norms = gain_norms + (gain_norms[0] / gain_norms[1],)
    new_gains = norm_gains - RATE * gain_norms[2][:, None] * gain_update
    note(At.new_gateup, new_gateup)
    note(At.new_down, new_down)
    note(At.new_gains, new_gains)

    *out_new, out_sq = lamb_turned(out_grads, moment_out, second_out, w_out, n_z, "lamb_out")
    note(At.lamb_out, out_sq)
    *qkv_new, qkv_sq = lamb_qkv(
        hold(At.lamb_qkv, qkv_grads),
        (moment_query, second_query, w_query),
        (moment_keyval, second_keyval, w_keyval),
    )
    attn_sq = all_sum(jnp.concatenate([qkv_sq, out_sq[None]]).reshape(-1, 128))
    new_query, new_keyval, new_out, norms = attn_step(
        attn_sq.reshape(4, 2, 8, 128),
        (w_query, qkv_new[1], qkv_new[2]),
        (w_keyval, qkv_new[4], qkv_new[5]),
        (w_out, out_new[1], out_new[2]),
    )
    attn_norms = norms[:3, :4]
    results = (qkv_new[:3], qkv_new[3:], out_new, gateup_new, down_new)
    grad_parts = tuple((entry[0] for entry in results))
    new_moments = tuple((entry[1] for entry in results))
    new_seconds = tuple((entry[2] for entry in results))
    new_parts = (new_query, new_keyval, new_out, new_gateup, new_down)
    weight_norms, update_norms, trust_ratios = (
        jnp.concatenate([attn_norms[at], ffn_norms[at], gain_norms[at]]) for at in range(3)
    )
    return (
        block_out,
        input_grad[None],
        grad_gains,
        grad_parts[0],
        grad_parts[1],
        grad_parts[2],
        grad_parts[3],
        grad_parts[4],
        new_gains,
        new_parts[0],
        new_parts[1],
        new_parts[2],
        new_parts[3],
        new_parts[4],
        gain_moment,
        new_moments[0],
        new_moments[1],
        new_moments[2],
        new_moments[3],
        new_moments[4],
        gain_second,
        new_seconds[0],
        new_seconds[1],
        new_seconds[2],
        new_seconds[3],
        new_seconds[4],
        weight_norms,
        update_norms,
        trust_ratios,
    )


def solution(mesh):
    n_dp, n_tensor = mesh.devices.shape
    split = jax.sharding.Mesh(
        mesh.devices.reshape(n_dp // 8, 4, 2, n_tensor // 2, 2), ("o", "z", "x", "y", "c")
    )
    dp, tensor = ("o", "z", "x"), ("y", "c")
    in_specs = (
        P(dp, tensor, None),
        P(dp, tensor, None),
        P(dp, None),
        P(),
        P(dp, tensor),
        P(None, dp, tensor),
        P(tensor, dp),
        P(None, dp, tensor),
        P(tensor, dp),
        P(),
        P(dp, tensor),
        P(None, dp, tensor),
        P(tensor, dp),
        P(None, dp, tensor),
        P(tensor, dp),
        P(),
        P(dp, tensor),
        P(None, dp, tensor),
        P(tensor, dp),
        P(None, dp, tensor),
        P(tensor, dp),
    )
    out_specs = (
        P(dp, tensor, None),
        P(dp, tensor, None),
        P(),
        P(dp, tensor),
        P(None, dp, tensor),
        P(tensor, dp),
        P(None, dp, tensor),
        P(tensor, dp),
        P(),
        P(dp, tensor),
        P(None, dp, tensor),
        P(tensor, dp),
        P(None, dp, tensor),
        P(tensor, dp),
        P(),
        P(dp, tensor),
        P(None, dp, tensor),
        P(tensor, dp),
        P(None, dp, tensor),
        P(tensor, dp),
        P(),
        P(dp, tensor),
        P(None, dp, tensor),
        P(tensor, dp),
        P(None, dp, tensor),
        P(tensor, dp),
        P(),
        P(),
        P(),
    )
    return jax.shard_map(
        per_device, mesh=split, in_specs=in_specs, out_specs=out_specs, check_vma=False
    )
```

```python
import jax
import jax.numpy as jnp
import numpy as np
from jax import lax
from jax.experimental import pallas as pl
from jax.experimental.pallas import tpu as pltpu
from jax.sharding import PartitionSpec as P

HD = 64


EPS_NORM = 1e-05
BETA = 0.5
LAMB_EPS = 1e-06
DECAY = 0.01
RATE = 0.5
NEG_FILL = -1e30


def rope_inverse(half_dim):
    exponent = np.arange(half_dim, dtype=np.float32) * np.float32(2.0 / (2 * half_dim))
    base_freq = np.float32(1.0) / np.power(np.float32(500000.0), exponent)
    wave_len = np.float32(2.0 * np.pi) / base_freq
    smooth = (np.float32(8192.0) / wave_len - np.float32(1.0)) / np.float32(3.0)
    middle = (np.float32(1.0) - smooth) * base_freq / np.float32(32.0) + smooth * base_freq
    scaled = np.where(
        wave_len < 2048.0,
        base_freq,
        np.where(wave_len > 8192.0, base_freq / np.float32(32.0), middle),
    )
    return scaled.astype(np.float32)


def doc_layout(lengths, position):
    doc_ends = jnp.cumsum(lengths, dtype=jnp.int32)
    starts_at = doc_ends - lengths
    segment = jnp.sum(
        (position[:, None] >= doc_ends[None, :]).astype(jnp.int32), axis=1, dtype=jnp.int32
    )
    onehot_doc = (
        segment[:, None] == jnp.arange(lengths.shape[0], dtype=jnp.int32)[None, :]
    ).astype(jnp.int32)
    doc_place = position - jnp.sum(onehot_doc * starts_at[None, :], axis=1, dtype=jnp.int32)
    return (segment, doc_place)


def rope_tables(doc_place, head_dim):
    inverse = jnp.asarray(rope_inverse(head_dim // 2))
    angles = doc_place.astype(jnp.float32)[:, None] * inverse[None, :]
    return (jnp.cos(angles), jnp.sin(angles))


def rounded(value):
    return value.astype(jnp.bfloat16)


def widened(value):
    return value.astype(jnp.float32)


def dot_plain(left_side, right_side):
    return lax.dot_general(
        left_side, right_side, (((1,), (0,)), ((), ())), preferred_element_type=jnp.float32
    )


def dot_rows(left_side, right_side):
    return lax.dot_general(
        left_side, right_side, (((1,), (1,)), ((), ())), preferred_element_type=jnp.float32
    )


def dot_cols(left_side, right_side):
    return lax.dot_general(
        left_side, right_side, (((0,), (0,)), ((), ())), preferred_element_type=jnp.float32
    )


class At:
    (
        wqkv_z1,
        wqkv_z2,
        wqkv_x0,
        wqkv_z3,
        wqkv_x1,
        wqkv_x2,
        pack,
        tables,
        cosine,
        sine,
        wout_z1,
        wout_z2,
        wout_x0,
        wqkv_x3,
        a_y,
        a_c,
        wout_z3,
        wout_x1,
        wout_x2,
        wout_x3,
        wgu_z,
        attend,
        mid_c,
        mid_add,
        mid_y,
        pair,
        bd_z2,
        bd_z1,
        wgu_x,
        wd_z,
        wd_x,
        bd_z3,
        bd0_y,
        bd0_c,
        bd1_y,
        bd1_c,
        bd2_y,
        bd2_c,
        bd3_y,
        bd3_c,
        ffn0,
        ffn1,
        ffn2,
        ffn3,
        db0_c,
        db0_add,
        db0_y,
        db1_c,
        db1_add,
        db1_y,
        db2_c,
        db2_add,
        db2_y,
        db3_c,
        db3_add,
        db3_y,
        db1_z,
        db3_z,
        db2_z,
        gdown,
        gdown_x,
        gdown_own,
        ggu,
        ggu_x,
        ggu_own,
        gqkv,
        gqkv_x,
        gqkv_own,
        gout,
        gout_x,
        gout_own,
        out_rows,
        gdown_z,
        out_c,
        out_add,
        ffnin,
        dmid_y,
        dmid_c,
        out_y,
        ggu_z,
        dmid,
        attend_back,
        lamb_down,
        grad_rows,
        da_c,
        da_add,
        da_y,
        out_z,
        lamb_gateup,
        gout_z,
        input_grad,
        gqkv_z,
        block_out,
        sums,
        new_gateup,
        new_down,
        new_gains,
        lamb_out,
        lamb_qkv,
        swap,
    ) = range(100)


GATES = {
    At.wqkv_z3: (At.wqkv_z1, At.wqkv_x0),
    At.wqkv_x1: (At.wqkv_x0,),
    At.wqkv_x2: (At.wqkv_z2,),
    At.a_y: (At.wqkv_z2, At.wqkv_x0),
    At.wout_z1: (At.wqkv_z3, At.wqkv_x1, At.wqkv_x2, At.a_y, At.pack, At.tables, At.cosine, At.sine),
    At.wout_z2: (At.wqkv_z3, At.wqkv_x1, At.wqkv_x2, At.a_y, At.pack, At.tables, At.cosine, At.sine),
    At.wout_x0: (At.wqkv_z3, At.wqkv_x1, At.wqkv_x2, At.a_y, At.pack, At.tables, At.cosine, At.sine),
    At.wqkv_x3: (At.wqkv_z3, At.wqkv_x1, At.wqkv_x2, At.a_y, At.pack, At.tables, At.cosine),
    At.a_c: (At.wqkv_z3, At.wqkv_x1, At.wqkv_x2, At.a_y, At.pack, At.tables, At.cosine, At.sine),
    At.wout_z3: (At.wout_z2, At.wout_x0),
    At.wout_x1: (At.wout_z1, At.wout_z2, At.wout_x0, At.wqkv_x3, At.wqkv_x1),
    At.wout_x2: (At.wout_z2, At.wout_x0, At.wqkv_x3),
    At.wgu_z: (At.wout_z3, At.pack),
    At.pair: (At.wgu_z,),
    At.wd_x: (At.wgu_x,),
    At.bd_z3: (At.wout_z3,),
    At.bd1_y: (At.bd0_y,),
    At.ffn0: (At.bd_z1,),
    At.bd2_y: (At.bd_z1,),
    At.ffn1: (At.bd_z3, At.ffn0),
    At.bd2_c: (At.ffn1,),
    At.bd3_y: (At.ffn0,),
    At.db1_add: (At.bd3_y, At.db2_c, At.ffn2, At.db0_c),
    At.db2_add: (At.bd3_y,),
    At.gdown: (At.db3_c,),
    At.ggu: (At.gdown,),
    At.gdown_own: (At.out_rows, At.db0_y),
    At.ggu_own: (At.gdown_x,),
    At.db3_z: (At.db1_z,),
    At.db2_z: (At.gdown_x,),
    At.ffnin: (At.gdown_x,),
    At.attend_back: (At.out_add,),
    At.gout: (At.gqkv_x,),
    At.out_z: (At.lamb_down, At.gqkv),
    At.gout_z: (At.out_z, At.lamb_down),
    At.gqkv_z: (At.gout_z,),
    At.lamb_down: (At.gqkv,),
    At.gqkv_own: (At.gqkv, At.gout),
    At.gout_own: (At.gout,),
    At.lamb_qkv: (At.new_gateup, At.new_down, At.new_gains, At.lamb_out, At.block_out, At.input_grad, At.gout_own, At.da_c),
    At.sums: (At.gqkv_own,),
    At.bd_z1: (At.mid_y,),
    At.out_add: (At.gdown_z, At.gdown),
    At.ffn2: (At.bd3_y, At.bd_z3),
    At.wgu_x: (At.a_c,),
    At.gqkv: (At.gdown_z,),
    At.bd0_c: (At.bd_z1,),
    At.out_c: (At.ffn3,),
    At.wout_x3: (At.a_y,),
}
MADE = {}


def note(what, value):
    MADE[what] = value
    return value


def hold(what, value):
    waits = [MADE[name] for name in GATES.get(what, ()) if name in MADE]
    return after(value, *waits) if waits else value


def exchange(value, axis, mask, what=At.swap):
    names = axis if isinstance(axis, tuple) else (axis,)
    size = 1
    for name in names:
        size = size * lax.axis_size(name)
    pairs = [(place, place ^ mask) for place in range(size)]
    return note(what, lax.ppermute(hold(what, value), axis, pairs))


def resplit(value, what):
    return note(what, lax.all_to_all(hold(what, value), "z", 0, 0, tiled=True))


def after(value, *others):
    return lax.optimization_barrier((value,) + others)[0]


def gather_row(value, what):
    across = exchange(value, "y", 1, what)
    return gather_core(value, across, what)


def gather_core(value, across, what, *waits):
    pair = jnp.concatenate([value, after(across, *waits)])
    return (value, across, exchange(pair, "c", 1, what + 1))


class RowSum:
    def __init__(self, keep, send, what):
        self.keep, self.what = keep, what
        self.tokens = keep.shape[0] // 2
        self.received = exchange(send, "c", 1, what)

    def pass_on(self):
        tokens = self.tokens
        received = hold(self.what + 1, self.received)
        passed = rounded(widened(self.keep[tokens:]) + widened(received[tokens:]))
        self.across = exchange(passed, "y", 1, self.what + 2)

    def total(self):
        tokens = self.tokens
        return (
            widened(self.keep[:tokens])
            + widened(self.received[:tokens])
            + widened(self.across)
        )


def scatter_row(keep, send, what):
    row = RowSum(keep, send, what)
    row.pass_on()
    return row.total()


def all_sum(value):
    for axis in ("c", "z", "x", "y", "o"):
        mask = 1
        while mask < lax.axis_size(axis):
            value = value + exchange(value, axis, mask)
            mask = mask * 2
    return value


HBM = pl.BlockSpec(memory_space=pl.ANY)
VMEM = pl.BlockSpec(memory_space=pltpu.VMEM)
SMEM = pl.BlockSpec(memory_space=pltpu.SMEM)


def start_copies(pairs, sems, first=0):
    copies = [
        pltpu.make_async_copy(source, target, sems.at[first + place])
        for place, (source, target) in enumerate(pairs)
    ]
    for copy in copies:
        copy.start()
    return copies


def row_copies(pieces, target):
    pairs, first = [], 0
    for piece in pieces:
        pairs.append((piece, target.at[pl.ds(first, piece.shape[0]), :]))
        first += piece.shape[0]
    return pairs


def block_rows_of(index, place, depth):
    return pl.ds(pl.multiple_of(index[place] * depth, depth), depth)


def lane_iota(rows):
    return lax.broadcasted_iota(jnp.int32, (rows, 128), 1)


def partner(value):
    lane = lane_iota(value.shape[0])
    return jnp.where(lane % HD < HD // 2, pltpu.roll(value, 128 - HD // 2, 1), pltpu.roll(value, HD // 2, 1))


def head_lanes(value, head, kv):
    lane = lane_iota(value.shape[0])
    moved = value if head % 2 == kv else pltpu.roll(value, HD, 1)
    keep = lane < HD if kv == 0 else lane >= HD
    return jnp.where(keep, moved, 0.0)


def pair_slab(even, odd, kv):
    lane = lane_iota(even.shape[0])
    if kv == 0:
        odd = pltpu.roll(odd, HD, 1)
    else:
        even = pltpu.roll(even, HD, 1)
    return jnp.where(lane < HD, even, odd)


CHUNK = 256


def attend_body(n_blocks, heads, group, *refs):
    index, a_own, a_across, a_core = refs[:4]
    weights = refs[4 : 4 + n_blocks]
    cosine, sine, bias = refs[4 + n_blocks : 7 + n_blocks]
    a_all, q_out, kv_out, ctx_out, lse_out = refs[7 + n_blocks : 12 + n_blocks]
    held, sems = refs[12 + n_blocks :]
    depth = weights[0].shape[0]
    copies = start_copies(row_copies((a_own, a_across, a_core), a_all), sems)
    copies += start_copies(
        [
            (weights[i].at[:, : held.shape[1]], held.at[block_rows_of(index, i, depth), :])
            for i in range(n_blocks)
        ],
        sems,
        3,
    )
    for copy in copies:
        copy.wait()
    rows_all = a_all.shape[0]
    n_slabs = heads // 2

    @pl.loop(0, rows_all // CHUNK)
    def _(at):
        rows = pl.ds(pl.multiple_of(at * CHUNK, CHUNK), CHUNK)
        raw = dot_plain(a_all[rows, :], held[...])
        cos, sin = cosine[rows, :], sine[rows, :]
        for slab in range(n_slabs + 1):
            part = raw[:, slab * 128 : (slab + 1) * 128]
            part = part * cos + partner(part) * sin
            if slab < n_slabs:
                for head in (2 * slab, 2 * slab + 1):
                    q_out[head, rows, :] = rounded(head_lanes(part, head, head // group))
            else:
                kv_out[0, rows, :] = rounded(part)
        kv_out[1, rows, :] = rounded(raw[:, (n_slabs + 1) * 128 : (n_slabs + 2) * 128])

    @pl.loop(0, rows_all // CHUNK)
    def _(at):
        rows = pl.ds(pl.multiple_of(at * CHUNK, CHUNK), CHUNK)
        keys, values = kv_out[0], kv_out[1]
        lane = lane_iota(CHUNK)
        logs = jnp.zeros((CHUNK, 128), jnp.float32)
        for slab in range(n_slabs):
            outs = []
            for head in (2 * slab, 2 * slab + 1):
                scores = dot_rows(q_out[head, rows, :], keys) * HD ** (-0.5) + bias[rows, :]
                most = jnp.max(scores, axis=-1, keepdims=True)
                shifted = jnp.exp(scores - most)
                total = jnp.sum(shifted, axis=-1, keepdims=True)
                outs.append(dot_plain(rounded(shifted / total), values))
                logs = jnp.where(lane == head, most + jnp.log(total), logs)
            ctx_out[rows, slab * 128 : (slab + 1) * 128] = rounded(
                pair_slab(outs[0], outs[1], 2 * slab // group)
            )
        lse_out[rows, :] = logs


def attend_back_body(n_blocks, heads, group, *refs):
    index, d_all = refs[:2]
    weights = refs[2 : 2 + n_blocks]
    queries, keyvals, bias, logs, cosine, sine = refs[2 + n_blocks : 8 + n_blocks]
    out = refs[8 + n_blocks]
    held, d_heads, key_sum, value_sum, sems = refs[9 + n_blocks :]
    depth, wide = weights[0].shape[0], held.shape[1]
    first = weights[0].shape[1] - wide
    copies = start_copies(
        [
            (weights[i].at[:, pl.ds(first, wide)], held.at[block_rows_of(index, i, depth), :])
            for i in range(n_blocks)
        ],
        sems,
    )
    for copy in copies:
        copy.wait()
    rows_all = d_all.shape[0]
    n_slabs = heads // 2
    key_sum[...] = jnp.zeros_like(key_sum)
    value_sum[...] = jnp.zeros_like(value_sum)

    @pl.loop(0, rows_all // CHUNK)
    def _(at):
        rows = pl.ds(pl.multiple_of(at * CHUNK, CHUNK), CHUNK)
        d_ctx = dot_plain(d_all[rows, :], held[...])
        for slab in range(n_slabs):
            part = d_ctx[:, slab * 128 : (slab + 1) * 128]
            for head in (2 * slab, 2 * slab + 1):
                d_heads[head, :, :] = rounded(head_lanes(part, head, head // group))
        keys, values = keyvals[0], keyvals[1]
        lane = lane_iota(CHUNK)
        cos, sin = cosine[rows, :], sine[rows, :]
        log_rows = logs[rows, :]
        for slab in range(n_slabs):
            kv = 2 * slab // group
            outs = []
            for head in (2 * slab, 2 * slab + 1):
                query, d_head = queries[head, rows, :], d_heads[head]
                log_total = jnp.sum(jnp.where(lane == head, log_rows, 0.0), axis=-1, keepdims=True)
                scores = dot_rows(query, keys) * HD ** (-0.5) + bias[rows, :]
                probs = jnp.exp(scores - log_total)
                d_probs = dot_rows(d_head, values)
                inner = jnp.sum(probs * d_probs, axis=-1, keepdims=True)
                d_scores = rounded(probs * (d_probs - inner) * HD ** (-0.5))
                key_sum[...] += dot_cols(d_scores, query)
                value_sum[...] += dot_cols(rounded(probs), d_head)
                outs.append(dot_plain(d_scores, keys))
            part = pair_slab(outs[0], outs[1], kv)
            out[rows, slab * 128 : (slab + 1) * 128] = rounded(part * cos - partner(part) * sin)

    key_grad = key_sum[...]
    key_grad = key_grad * cosine[...] - partner(key_grad) * sine[...]
    out[:, n_slabs * 128 : (n_slabs + 1) * 128] = rounded(key_grad)
    out[:, (n_slabs + 1) * 128 : (n_slabs + 2) * 128] = rounded(value_sum[...])


def rows_out_body(n_blocks, first, *refs):
    index, left = refs[:2]
    weights = refs[2 : 2 + n_blocks]
    keep, send, held, sems = refs[2 + n_blocks :]
    depth, wide = weights[0].shape[0], held.shape[1]
    copies = start_copies(
        [
            (weights[i].at[:, pl.ds(first, wide)], held.at[block_rows_of(index, i, depth), :])
            for i in range(n_blocks)
        ],
        sems,
    )
    for copy in copies:
        copy.wait()
    half = left.shape[0] // 2
    send[...] = rounded(dot_rows(left[half:, :], held[...]))
    keep[...] = rounded(dot_rows(left[:half, :], held[...]))


def natural_rows(scalars, pieces, which, target):
    tokens = pieces[0].shape[0] // 2
    pairs = []
    for at in range(4):
        place = pl.ds(pl.multiple_of(scalars[3 + at] * tokens, tokens), tokens)
        piece = pieces[min(at, 2)]
        first = (which + 2 * (at - 2 if at > 2 else 0)) * tokens
        pairs.append((piece.at[pl.ds(first, tokens), :], target.at[place, :]))
    return pairs


def ffn_body(n_parts, n_z, n_alias, scalars, *refs):
    pieces = refs[:3]
    gateup = refs[3 : 3 + n_parts]
    down = refs[3 + n_parts : 3 + 2 * n_parts]
    refs = refs[3 + 2 * n_parts + n_alias :]
    b_all, d_all, hid, grad_pair, keep, send, b_rows, d_rows, wide, deep, sems = refs
    first = pl.multiple_of(scalars[0] * b_rows.shape[0], b_rows.shape[0])
    own_rows = pl.ds(first, b_rows.shape[0])
    last = sems.shape[0] - 2
    part = down[0].shape[2]
    copies = start_copies(natural_rows(scalars, pieces, 0, b_rows), sems)
    copies += start_weights(scalars, 7, gateup, (), wide, None, sems, 4)
    later = start_copies(natural_rows(scalars, pieces, 1, d_rows), sems, len(copies))
    later += start_weights(scalars, 7, (), down, None, deep, sems, len(copies) + 4)
    for copy in copies:
        copy.wait()
    kept = start_copies([(b_rows, b_all.at[own_rows, :])], sems, last)
    pre = dot_plain(b_rows[...], wide[...])
    for copy in later:
        copy.wait()
    kept += start_copies([(d_rows, d_all.at[own_rows, :])], sems, last + 1)
    d_hid = dot_plain(d_rows[...], deep[...])
    gate_pre, up_pre = pre[:, :part], pre[:, part:]
    sigma = jax.nn.sigmoid(gate_pre)
    silu = gate_pre * sigma
    hid[...] = rounded(silu * up_pre)
    d_gate = d_hid * up_pre * (sigma * (1.0 + gate_pre * (1.0 - sigma)))
    grad_pair[:, :part] = rounded(d_gate)
    grad_pair[:, part:] = rounded(d_hid * silu)
    grad_in = rounded(dot_rows(grad_pair[...], wide[...]))
    lay_out(grad_in, scalars, keep, send)
    for copy in kept:
        copy.wait()


def start_weights(index, first, gateup, down, wide, deep, sems, first_sem=0):
    pairs = []
    for i, piece in enumerate(gateup):
        n_z, _, depth, part = piece.shape
        for z in range(n_z):
            block = block_rows_of(index, first + i * n_z + z, depth)
            for half in range(2):
                pairs.append((piece.at[z, half], wide.at[block, pl.ds(half * part, part)]))
    for i, piece in enumerate(down):
        n_z, depth, _ = piece.shape
        for z in range(n_z):
            pairs.append((piece.at[z], deep.at[block_rows_of(index, first + i * n_z + z, depth), :]))
    return start_copies(pairs, sems, first_sem)


def cost(flops, nbytes):
    return pl.CostEstimate(flops=flops, bytes_accessed=nbytes, transcendentals=0)


def bf16_of(*shape):
    return jax.ShapeDtypeStruct(shape, jnp.bfloat16)


def attend(index, pieces, weights, cosine, sine, bias, heads, group):
    rows, width = cosine.shape[0], pieces[0].shape[1]
    n_blocks, wide = len(weights), (heads + 4) * HD
    return pl.pallas_call(
        lambda *refs: attend_body(n_blocks, heads, group, *refs),
        out_shape=(
            bf16_of(rows, width),
            bf16_of(heads, rows, 128),
            bf16_of(2, rows, 128),
            bf16_of(rows, heads * HD),
            jax.ShapeDtypeStruct((rows, 128), jnp.float32),
        ),
        in_specs=[SMEM] + [HBM] * (3 + n_blocks) + [VMEM] * 3,
        out_specs=(VMEM,) * 5,
        scratch_shapes=[
            pltpu.VMEM((width, wide), jnp.bfloat16),
            pltpu.SemaphoreType.DMA((3 + n_blocks,)),
        ],
        cost_estimate=cost(2 * rows * width * wide + 4 * heads * rows * rows * 128, 8 << 20),
        name="attend",
    )(index, *pieces, *weights, cosine, sine, bias)


def attend_back(index, grad_rows, weights, queries, keyvals, bias, logs, cosine, sine, heads, group):
    rows, width = grad_rows.shape
    n_blocks, wide = len(weights), heads * HD
    return pl.pallas_call(
        lambda *refs: attend_back_body(n_blocks, heads, group, *refs),
        out_shape=bf16_of(rows, heads * HD + 256),
        in_specs=[SMEM, VMEM] + [HBM] * n_blocks + [VMEM] * 6,
        out_specs=VMEM,
        scratch_shapes=[
            pltpu.VMEM((width, wide), jnp.bfloat16),
            pltpu.VMEM((heads, CHUNK, 128), jnp.bfloat16),
            pltpu.VMEM((rows, 128), jnp.float32),
            pltpu.VMEM((rows, 128), jnp.float32),
            pltpu.SemaphoreType.DMA((n_blocks,)),
        ],
        cost_estimate=cost(2 * rows * width * wide + 10 * heads * rows * rows * 128, 8 << 20),
        name="attend_back",
    )(index, grad_rows, *weights, queries, keyvals, bias, logs, cosine, sine)


def rows_out(index, left, weights, first, name):
    rows, wide = left.shape
    n_blocks = len(weights)
    width = n_blocks * weights[0].shape[0]
    return pl.pallas_call(
        lambda *refs: rows_out_body(n_blocks, first, *refs),
        out_shape=(bf16_of(rows // 2, width),) * 2,
        in_specs=[SMEM, VMEM] + [HBM] * n_blocks,
        out_specs=(VMEM,) * 2,
        scratch_shapes=[
            pltpu.VMEM((width, wide), jnp.bfloat16),
            pltpu.SemaphoreType.DMA((n_blocks,)),
        ],
        cost_estimate=cost(2 * rows * width * wide, 6 << 20),
        name=name,
    )(index, left, *weights)


def ffn_rows(scalars, pieces, gateup, down, total, earlier):
    row_len, width = 2 * pieces[0].shape[0], pieces[0].shape[1]
    n_parts, n_z, part = len(gateup), gateup[0].shape[0], gateup[0].shape[3]
    n_alias = len(earlier)

    def block(wide):
        return pl.BlockSpec((row_len, wide), lambda i, scalars: (scalars[0], 0))

    def whole(wide):
        return pl.BlockSpec((row_len // 2, wide), lambda i, scalars: (0, 0))

    return pl.pallas_call(
        lambda *refs: ffn_body(n_parts, n_z, n_alias, *refs),
        grid_spec=pltpu.PrefetchScalarGridSpec(
            num_scalar_prefetch=1,
            grid=(1,),
            in_specs=[HBM] * (3 + 2 * n_parts + n_alias),
            out_specs=(HBM, HBM, block(part), block(2 * part), whole(width), whole(width)),
            scratch_shapes=[
                pltpu.VMEM((row_len, width), jnp.bfloat16),
                pltpu.VMEM((row_len, width), jnp.bfloat16),
                pltpu.VMEM((width, 2 * part), jnp.bfloat16),
                pltpu.VMEM((width, part), jnp.bfloat16),
                pltpu.SemaphoreType.DMA((10 + 3 * n_parts * n_z,)),
            ],
        ),
        out_shape=(
            bf16_of(total, width),
            bf16_of(total, width),
            bf16_of(total, part),
            bf16_of(total, 2 * part),
            bf16_of(row_len // 2, width),
            bf16_of(row_len // 2, width),
        ),
        input_output_aliases={4 + 2 * n_parts + at: at for at in range(n_alias)},
        cost_estimate=cost(row_len * width, 1 << 20),
        name="ffn_rows",
    )(scalars, *pieces, *gateup, *down, *earlier)


def weight_grad_body(index, left, right, out):
    out[0] = rounded(dot_cols(left[...], right[...]))


def weight_grad(index, part, left, right, depth, count):
    rows, wide = right.shape
    if depth % 128:
        blocks = rounded(dot_cols(left, right)).reshape(-1, depth, wide)
        return blocks[index[part * count : (part + 1) * count]]
    return pl.pallas_call(
        weight_grad_body,
        grid_spec=pltpu.PrefetchScalarGridSpec(
            num_scalar_prefetch=1,
            grid=(count,),
            in_specs=[
                pl.BlockSpec((rows, depth), lambda i, index: (0, index[part * count + i])),
                pl.BlockSpec((rows, wide), lambda i, index: (0, 0)),
            ],
            out_specs=pl.BlockSpec((1, depth, wide), lambda i, index: (i, 0, 0)),
        ),
        out_shape=bf16_of(count, depth, wide),
        cost_estimate=cost(rows * wide, 1 << 20),
        name="weight_grad",
    )(index, left, right)


def lay_out(value, scalars, keep, send, lead=()):
    tokens = value.shape[0] // 4
    for place in range(4):
        piece = value[place * tokens : (place + 1) * tokens, :]
        target = pl.ds(pl.multiple_of(((place // 2) ^ scalars[1]) * tokens, tokens), tokens)

        @pl.when(scalars[2] == place % 2)
        def _():
            keep[(*lead, target, slice(None))] = piece

        @pl.when(scalars[2] != place % 2)
        def _():
            send[(*lead, target, slice(None))] = piece


def out_rows_body(n_parts, scalars, left, *refs):
    down = refs[:n_parts]
    keep, send, deep, sems = refs[n_parts:]

    @pl.when(pl.program_id(0) == 0)
    def _():
        for copy in start_weights(scalars, 7, (), down, None, deep, sems):
            copy.wait()

    lay_out(rounded(dot_rows(left[...], deep[...])), scalars, keep, send, (0,))


def out_rows(scalars, left, down, row_len):
    rows, part = left.shape
    n_parts, n_z, depth = len(down), down[0].shape[0], down[0].shape[1]
    width, n_rows = n_parts * n_z * depth, rows // row_len
    block = pl.BlockSpec((1, row_len // 2, width), lambda i, scalars: (i, 0, 0))
    return pl.pallas_call(
        lambda *refs: out_rows_body(n_parts, *refs),
        grid_spec=pltpu.PrefetchScalarGridSpec(
            num_scalar_prefetch=1,
            grid=(n_rows,),
            in_specs=[pl.BlockSpec((row_len, part), lambda i, scalars: (i, 0))] + [HBM] * n_parts,
            out_specs=(block, block),
            scratch_shapes=[
                pltpu.VMEM((width, part), jnp.bfloat16),
                pltpu.SemaphoreType.DMA((n_parts * n_z,)),
            ],
        ),
        out_shape=(bf16_of(n_rows, row_len // 2, width),) * 2,
        cost_estimate=cost(rows * width, 1 << 20),
        name="out_rows",
    )(scalars, left, *down)


def lamb_update(gradient, moment, second, weight):
    new_moment = BETA * moment + (1.0 - BETA) * gradient
    new_second = BETA * second + (1.0 - BETA) * gradient * gradient
    update = new_moment / (jnp.sqrt(new_second) + LAMB_EPS) + DECAY * weight
    return (new_moment, new_second, update)


def tile_sum(value):
    rows, wide = value.shape
    step = min(wide, 128)
    total = value[:, :step]
    for at in range(1, wide // step):
        total = total + value[:, at * step : (at + 1) * step]
    return jnp.sum(total.reshape(rows // 8, 8, step), axis=0)


def lamb_step(gradient, refs, place):
    moment, second, weight, grad_out, moment_out, second_out = refs
    new_moment, new_second, update = lamb_update(
        gradient, moment[place], second[place], weight[place]
    )
    grad_out[place] = gradient
    moment_out[place] = new_moment
    second_out[place] = new_second
    return tile_sum(update * update), tile_sum(weight[place] * weight[place])


def lamb_gateup_body(grads, *refs):
    sums = refs[6]
    update_sq, weight_sq = lamb_step(widened(grads[0]), refs[:6], 0)

    @pl.when(pl.program_id(1) == 0)
    def _():
        sums[...] = jnp.zeros_like(sums)

    sums[0, 0] += update_sq
    sums[0, 1] += weight_sq


def lamb_gateup(grads, moment, second, weight):
    two, depth, held = weight.shape
    n_z, part = grads.shape[0], held // grads.shape[0]
    block = pl.BlockSpec((1, depth, part), lambda half, z: (half, 0, z))
    whole = jax.ShapeDtypeStruct(weight.shape, jnp.float32)
    return pl.pallas_call(
        lamb_gateup_body,
        grid=(two, n_z),
        in_specs=[pl.BlockSpec((1, depth, part), lambda half, z: (z, 0, half))] + [block] * 3,
        out_specs=(block,) * 3 + (pl.BlockSpec((1, 2, 8, 128), lambda half, z: (half, 0, 0, 0)),),
        out_shape=(whole,) * 3 + (jax.ShapeDtypeStruct((two, 2, 8, 128), jnp.float32),),
        cost_estimate=cost(20 * weight.size, 26 * weight.size),
        name="lamb_gateup",
    )(grads, moment, second, weight)


def lamb_turned_body(n_sum, grads, *refs):
    sums = refs[6]
    gradient = widened(grads[0])
    for at in range(1, n_sum):
        gradient = gradient + widened(grads[at])
    update_sq, weight_sq = lamb_step(gradient.T, refs[:6], ...)

    @pl.when(pl.program_id(0) == 0)
    def _():
        sums[...] = jnp.zeros_like(sums)

    step = update_sq.shape[1]
    sums[0, :, :step] += update_sq
    sums[1, :, :step] += weight_sq


def lamb_turned(grads, moment, second, weight, n_sum, name):
    rows, depth = grads.shape[2], grads.shape[1]
    block = pl.BlockSpec((rows, depth), lambda i: (i, 0))
    whole = jax.ShapeDtypeStruct(weight.shape, jnp.float32)
    return pl.pallas_call(
        lambda *refs: lamb_turned_body(n_sum, *refs),
        grid=(weight.shape[0] // rows,),
        in_specs=[pl.BlockSpec((n_sum, depth, rows), lambda i: (i, 0, 0))] + [block] * 3,
        out_specs=(block,) * 3 + (pl.BlockSpec((2, 8, 128), lambda i: (0, 0, 0)),),
        out_shape=(whole,) * 3 + (jax.ShapeDtypeStruct((2, 8, 128), jnp.float32),),
        cost_estimate=cost(20 * weight.size, 26 * weight.size),
        name=name,
    )(grads, moment, second, weight)


def lamb_qkv_body(grads, *refs):
    query, keyval, sums = refs[0:3] + refs[6:9], refs[3:6] + refs[9:12], refs[12]
    gradient = widened(grads[0])
    for at in range(1, grads.shape[0]):
        gradient = gradient + widened(grads[at])
    wide, narrow = query[0].shape[1], keyval[0].shape[2]
    sums[0, 0], sums[0, 1] = lamb_step(gradient[:, :wide], query, ...)
    for at in range(2):
        first = wide + at * narrow
        sums[1 + at, 0], sums[1 + at, 1] = lamb_step(
            gradient[:, first : first + narrow], keyval, at
        )


def lamb_qkv(grads, query, keyval):
    shapes = [jax.ShapeDtypeStruct(part[0].shape, jnp.float32) for part in (query, keyval)]
    return pl.pallas_call(
        lamb_qkv_body,
        in_specs=[VMEM] * 7,
        out_specs=(VMEM,) * 7,
        out_shape=(shapes[0],) * 3
        + (shapes[1],) * 3
        + (jax.ShapeDtypeStruct((3, 2, 8, 128), jnp.float32),),
        cost_estimate=cost(4 << 20, 6 << 20),
        name="lamb_qkv",
    )(grads, *query, *keyval)


def lamb_moments(gradient, moment, second):
    new_moment = BETA * moment + (1.0 - BETA) * gradient
    new_second = BETA * second + (1.0 - BETA) * gradient * gradient
    return (new_moment, new_second, new_moment / (jnp.sqrt(new_second) + LAMB_EPS))


def attn_step_body(sums, *refs):
    query, keyval, out = refs[0:3] + (refs[9],), refs[3:6] + (refs[10],), refs[6:9] + (refs[11],)
    norms = refs[12]
    lane = lane_iota(8)
    row = lax.broadcasted_iota(jnp.int32, (8, 128), 0)
    kept = jnp.zeros((8, 128), jnp.float32)
    targets = ((query, ...), (keyval, 0), (keyval, 1), (out, ...))
    for at, ((weight, moment, second, new), place) in enumerate(targets):
        update_norm, weight_norm = (
            jnp.sqrt(jnp.sum(jnp.sum(sums[at, which], axis=0, keepdims=True), axis=1, keepdims=True))
            for which in range(2)
        )
        ratio = weight_norm / update_norm
        for which, value in enumerate((weight_norm, update_norm, ratio)):
            kept = jnp.where((row == which) & (lane == at), value, kept)
        update = moment[place] / (jnp.sqrt(second[place]) + LAMB_EPS) + DECAY * weight[place]
        new[place] = weight[place] - RATE * (update * ratio)
    norms[...] = kept


def attn_step(sums, query, keyval, out):
    shapes = [jax.ShapeDtypeStruct(part[0].shape, jnp.float32) for part in (query, keyval, out)]
    return pl.pallas_call(
        attn_step_body,
        in_specs=[VMEM] * 10,
        out_specs=(VMEM,) * 4,
        out_shape=(*shapes, jax.ShapeDtypeStruct((8, 128), jnp.float32)),
        cost_estimate=cost(4 << 20, 6 << 20),
        name="attn_step",
    )(sums, *query, *keyval, *out)


def per_device(
    hidden_in,
    out_grad,
    doc_lengths,
    norm_gains,
    w_query,
    w_keyval,
    w_out,
    w_gateup,
    w_down,
    moment_gains,
    moment_query,
    moment_keyval,
    moment_out,
    moment_gateup,
    moment_down,
    second_gains,
    second_query,
    second_keyval,
    second_out,
    second_gateup,
    second_down,
):
    MADE.clear()
    tok = hidden_in.shape[1]
    width = hidden_in.shape[2]
    row_len = tok * 4
    n_o, n_z, n_x = lax.axis_size("o"), lax.axis_size("z"), lax.axis_size("x")
    n_parts = n_o * n_x
    depth = w_query.shape[0]
    heads_wide = w_query.shape[1]
    kv_wide = w_keyval.shape[2]
    local_heads = heads_wide // HD
    group_size = heads_wide // kv_wide
    ff_held = w_down.shape[0]
    ff_part = ff_held // n_z
    my_part = lax.axis_index("o") * n_x + lax.axis_index("x")
    my_z = lax.axis_index("z")

    part_of = my_part ^ jnp.arange(n_parts, dtype=jnp.int32)[:, None]
    z_of = jnp.arange(n_z, dtype=jnp.int32)[None, :]

    def block_of(part, z):
        return (((part // n_x) * n_z + z) * n_x + part % n_x).reshape(-1)

    y_at, c_at = lax.axis_index("y"), lax.axis_index("c")
    attn_index = block_of(part_of, my_z ^ z_of)
    ffn_index = block_of(part_of, z_of)

    token_block = [
        (y_at ^ y_other) * 2 + (c_at ^ c_other) for c_other in range(2) for y_other in range(2)
    ]

    def row_scalars(place):
        return jnp.concatenate([jnp.stack([my_z ^ place, y_at, c_at] + token_block), ffn_index])

    parts = range(1, n_parts)

    def to_parts(piece, what):
        return [exchange(piece, ("o", "x"), place, what) for place in parts]

    def in_order(column, across):
        return list(column) + [across[z][place - 1] for place in parts for z in range(n_z)]

    position = jnp.concatenate(
        [block * tok + jnp.arange(tok, dtype=jnp.int32) for block in token_block]
    )

    x_float = widened(hidden_in[0])
    gain_attn = norm_gains[0]
    gain_ffn = norm_gains[1]
    inv_one = lax.rsqrt(jnp.mean(x_float * x_float, axis=-1, keepdims=True) + EPS_NORM)
    normed_one = x_float * inv_one
    qkv_own = rounded(jnp.concatenate([w_query, w_keyval[0], w_keyval[1]], axis=1))
    qkv_near = exchange(qkv_own, "z", 1, At.wqkv_z1)
    qkv_far = exchange(qkv_own, "z", 2, At.wqkv_z2)
    qkv_x0 = to_parts(qkv_own, At.wqkv_x0)
    qkv_last = exchange(qkv_far, "z", 1, At.wqkv_z3)
    qkv_x1 = to_parts(qkv_near, At.wqkv_x1)
    qkv_x2 = to_parts(qkv_far, At.wqkv_x2)
    attn_own = rounded(normed_one * gain_attn)
    attn_across = exchange(attn_own, "y", 1, At.a_y)
    gateup_send = rounded(w_gateup).reshape(2, depth, n_z, ff_part).transpose(2, 0, 1, 3)
    note(At.pack, gateup_send)
    segment, doc_place = doc_layout(doc_lengths[0], position)
    cosine, sine_part = rope_tables(doc_place, HD)
    cosine = jnp.concatenate([cosine] * 4, axis=1)
    sine_part = jnp.concatenate([-sine_part, sine_part] * 2, axis=1)
    bias = jnp.where(
        (segment[:, None] == segment[None, :]) & (position[None, :] <= position[:, None]),
        jnp.float32(0.0),
        jnp.float32(NEG_FILL),
    )
    note(At.tables, bias)
    note(At.cosine, cosine)
    note(At.sine, sine_part)
    out_own = rounded(w_out.T)
    out_near = exchange(out_own, "z", 1, At.wout_z1)
    out_far = exchange(out_own, "z", 2, At.wout_z2)
    out_x0 = to_parts(out_own, At.wout_x0)
    qkv_x3 = to_parts(qkv_last, At.wqkv_x3)
    attn_pieces = gather_core(attn_own, attn_across, At.a_y)
    out_last = exchange(out_far, "z", 1, At.wout_z3)
    out_x1 = to_parts(out_near, At.wout_x1)
    out_x2 = to_parts(out_far, At.wout_x2)
    out_x3 = to_parts(out_last, At.wout_x3)
    qkv_w = in_order(
        (qkv_own, qkv_near, qkv_far, qkv_last), (qkv_x0, qkv_x1, qkv_x2, qkv_x3)
    )
    out_w = in_order(
        (out_own, out_near, out_far, out_last), (out_x0, out_x1, out_x2, out_x3)
    )
    gateup_own = resplit(gateup_send, At.wgu_z)
    attn_input, queries, keyvals, context, logs = attend(
        hold(At.attend, attn_index), attn_pieces, qkv_w, cosine, sine_part, bias, local_heads, group_size
    )
    mid_stream = x_float + scatter_row(
        *rows_out(attn_index, context, out_w, 0, "mid_rows"), At.mid_c
    )
    inv_two = lax.rsqrt(jnp.mean(mid_stream * mid_stream, axis=-1, keepdims=True) + EPS_NORM)
    normed_two = mid_stream * inv_two

    pair_own = jnp.concatenate(
        [rounded(normed_two * gain_ffn), hold(At.pair, out_grad[0])]
    )
    note(At.pair, pair_own)
    pair_far = exchange(pair_own, "z", 2, At.bd_z2)
    pair_near = exchange(pair_own, "z", 1, At.bd_z1)
    pair_across = exchange(pair_own, "y", 1, At.bd0_y)
    gateup_w = [gateup_own] + to_parts(gateup_own, At.wgu_x)
    down_turned = rounded(w_down).reshape(n_z, ff_part, depth).transpose(0, 2, 1)
    down_own = resplit(down_turned, At.wd_z)
    down_w = [down_own] + to_parts(down_own, At.wd_x)
    pair_last = exchange(pair_far, "z", 1, At.bd_z3)
    near_across = exchange(pair_near, "y", 1, At.bd1_y)
    pair_rows = {0: gather_core(pair_own, pair_across, At.bd0_y)}
    pair_rows[1] = gather_core(pair_near, near_across, At.bd1_y)
    held, rows = (), {}

    def ffn_row(place):
        *outs, keep, send = ffn_rows(
            hold(At.ffn0 + place, row_scalars(place)),
            pair_rows[place],
            gateup_w,
            down_w,
            n_z * row_len,
            held,
        )
        note(At.ffn0 + place, send)
        rows[place] = RowSum(keep, send, At.db0_c + 3 * place)
        return tuple(outs)

    held = ffn_row(0)
    far_across = exchange(pair_far, "y", 1, At.bd2_y)
    held = ffn_row(1)
    pair_rows[2] = gather_core(pair_far, far_across, At.bd2_y)
    last_across = exchange(pair_last, "y", 1, At.bd3_y)
    held = ffn_row(2)
    pair_rows[3] = gather_core(pair_last, last_across, At.bd3_y)
    for place in (1, 0, 2):
        rows[place].pass_on()
    held = ffn_row(3)
    rows[3].pass_on()
    ffn_input, grad_full, hidden_act, grad_pair = held

    def others(left, right, what):
        index = hold(what, ffn_index)
        made = [weight_grad(index, place, left, right, depth, n_z) for place in parts]
        note(what, made[-1])
        return [
            exchange(piece, ("o", "x"), place, what + 1) for place, piece in zip(parts, made)
        ]

    def with_own(left, right, moved, what):
        index = hold(what + 2, ffn_index)
        own = note(what + 2, weight_grad(index, 0, left, right, depth, n_z))
        total = widened(own)
        for piece in moved:
            total = total + widened(piece)
        return rounded(total)

    near_sum = exchange(rounded(rows[1].total()), "z", 1, At.db1_z)
    down_moves = others(grad_full, hidden_act, At.gdown)
    gateup_moves = others(ffn_input, grad_pair, At.ggu)
    last_sum = exchange(rounded(rows[3].total()), "z", 1, At.db3_z)
    far_sum = exchange(rounded(rows[2].total() + widened(last_sum)), "z", 2, At.db2_z)
    out_keep, out_send = out_rows(
        hold(At.out_rows, row_scalars(0)), hidden_act, down_w, row_len
    )
    note(At.out_rows, out_send)
    down_total = with_own(grad_full, hidden_act, down_moves, At.gdown)
    down_grads = resplit(down_total, At.gdown_z)
    out_received = exchange(out_send, "c", 1, At.out_c)
    out_passed = rounded(
        widened(out_keep[:, tok:]) + widened(hold(At.out_add, out_received)[:, tok:])
    )
    note(At.out_add, out_passed)
    grad_ffn_in = rows[0].total() + widened(near_sum) + widened(far_sum)
    grad_ffn_in = hold(At.ffnin, grad_ffn_in)

    gain_grad_ffn = jnp.sum(grad_ffn_in * normed_two, axis=0)
    grad_normed_two = grad_ffn_in * gain_ffn
    grad_mid = widened(out_grad[0]) + inv_two * (
        grad_normed_two
        - normed_two * jnp.mean(grad_normed_two * normed_two, axis=-1, keepdims=True)
    )
    grad_mid_rows = gather_row(rounded(grad_mid), At.dmid_y)
    out_across = exchange(out_passed, "y", 1, At.out_y)
    gateup_total = with_own(ffn_input, grad_pair, gateup_moves, At.ggu)
    gateup_grads = resplit(gateup_total, At.ggu_z)
    grad_mid_full = hold(At.dmid, jnp.concatenate(grad_mid_rows))
    grad_qkv = attend_back(
        hold(At.attend_back, attn_index),
        grad_mid_full,
        out_w,
        queries,
        keyvals,
        bias,
        logs,
        cosine,
        sine_part,
        local_heads,
        group_size,
    )
    note(At.attend_back, grad_qkv)
    qkv_moves = others(attn_input, grad_qkv, At.gqkv)
    out_moves = others(grad_mid_full, context, At.gout)
    *down_new, down_sq = lamb_turned(
        hold(At.lamb_down, down_grads), moment_down, second_down, w_down, 1, "lamb_down"
    )
    note(At.lamb_down, down_sq)
    grad_parts_send = rows_out(
        hold(At.grad_rows, attn_index), grad_qkv, qkv_w, 0, "grad_rows"
    )
    note(At.grad_rows, grad_parts_send[1])
    grad_attn_in = scatter_row(*grad_parts_send, At.da_c)
    out_total = rounded(
        widened(out_keep[:, :tok]) + widened(out_received[:, :tok]) + widened(out_across)
    )
    ffn_out = resplit(out_total, At.out_z)
    *gateup_new, gateup_sq = lamb_gateup(
        hold(At.lamb_gateup, gateup_grads), moment_gateup, second_gateup, w_gateup
    )
    note(At.lamb_gateup, gateup_sq)
    wout_total = with_own(grad_mid_full, context, out_moves, At.gout)
    qkv_total = with_own(attn_input, grad_qkv, qkv_moves, At.gqkv)
    out_grads = resplit(wout_total, At.gout_z)
    gain_grad_attn = jnp.sum(grad_attn_in * normed_one, axis=0)
    grad_normed_one = grad_attn_in * gain_attn
    input_grad = grad_mid + inv_one * (
        grad_normed_one
        - normed_one * jnp.mean(grad_normed_one * normed_one, axis=-1, keepdims=True)
    )
    note(At.input_grad, input_grad)
    qkv_grads = resplit(qkv_total, At.gqkv_z)
    block_out = rounded(mid_stream + jnp.sum(widened(ffn_out), axis=0))[None]
    note(At.block_out, block_out)
    gain_rows = 2 * width // 128
    packed = all_sum(
        hold(
            At.sums,
            jnp.concatenate(
                [gain_grad_attn.reshape(-1, 128), gain_grad_ffn.reshape(-1, 128)]
                + [gateup_sq.reshape(-1, 128), down_sq.reshape(-1, 128)]
            ),
        )
    )
    note(At.sums, packed)

    def ratios_of(totals):
        norms = jnp.sqrt(jnp.sum(totals.reshape(-1, 2, 1024), axis=2))
        return norms[:, 1], norms[:, 0], norms[:, 1] / norms[:, 0]

    def stepped(weight, entry, ratio):
        update = entry[1] / (jnp.sqrt(entry[2]) + LAMB_EPS) + DECAY * weight
        return weight - RATE * (update * ratio)

    ffn_norms = ratios_of(packed[gain_rows:])
    new_gateup = stepped(w_gateup, gateup_new, ffn_norms[2][:2][:, None, None])
    new_down = stepped(w_down, down_new, ffn_norms[2][2])
    grad_gains = packed[:gain_rows].reshape(2, width)
    gain_moment, gain_second, gain_direction = lamb_moments(grad_gains, moment_gains, second_gains)
    gain_update = gain_direction + DECAY * norm_gains
    gain_norms = (
        jnp.sqrt(jnp.sum(norm_gains * norm_gains, axis=1)),
        jnp.sqrt(jnp.sum(gain_update * gain_update, axis=1)),
    )
    gain_norms = gain_norms + (gain_norms[0] / gain_norms[1],)
    new_gains = norm_gains - RATE * gain_norms[2][:, None] * gain_update
    note(At.new_gateup, new_gateup)
    note(At.new_down, new_down)
    note(At.new_gains, new_gains)

    *out_new, out_sq = lamb_turned(out_grads, moment_out, second_out, w_out, n_z, "lamb_out")
    note(At.lamb_out, out_sq)
    *qkv_new, qkv_sq = lamb_qkv(
        hold(At.lamb_qkv, qkv_grads),
        (moment_query, second_query, w_query),
        (moment_keyval, second_keyval, w_keyval),
    )
    attn_sq = all_sum(jnp.concatenate([qkv_sq, out_sq[None]]).reshape(-1, 128))
    new_query, new_keyval, new_out, norms = attn_step(
        attn_sq.reshape(4, 2, 8, 128),
        (w_query, qkv_new[1], qkv_new[2]),
        (w_keyval, qkv_new[4], qkv_new[5]),
        (w_out, out_new[1], out_new[2]),
    )
    attn_norms = norms[:3, :4]
    results = (qkv_new[:3], qkv_new[3:], out_new, gateup_new, down_new)
    grad_parts = tuple((entry[0] for entry in results))
    new_moments = tuple((entry[1] for entry in results))
    new_seconds = tuple((entry[2] for entry in results))
    new_parts = (new_query, new_keyval, new_out, new_gateup, new_down)
    weight_norms, update_norms, trust_ratios = (
        jnp.concatenate([attn_norms[at], ffn_norms[at], gain_norms[at]]) for at in range(3)
    )
    return (
        block_out,
        input_grad[None],
        grad_gains,
        grad_parts[0],
        grad_parts[1],
        grad_parts[2],
        grad_parts[3],
        grad_parts[4],
        new_gains,
        new_parts[0],
        new_parts[1],
        new_parts[2],
        new_parts[3],
        new_parts[4],
        gain_moment,
        new_moments[0],
        new_moments[1],
        new_moments[2],
        new_moments[3],
        new_moments[4],
        gain_second,
        new_seconds[0],
        new_seconds[1],
        new_seconds[2],
        new_seconds[3],
        new_seconds[4],
        weight_norms,
        update_norms,
        trust_ratios,
    )


def solution(mesh):
    n_dp, n_tensor = mesh.devices.shape
    split = jax.sharding.Mesh(
        mesh.devices.reshape(n_dp // 8, 4, 2, n_tensor // 2, 2), ("o", "z", "x", "y", "c")
    )
    dp, tensor = ("o", "z", "x"), ("y", "c")
    in_specs = (
        P(dp, tensor, None),
        P(dp, tensor, None),
        P(dp, None),
        P(),
        P(dp, tensor),
        P(None, dp, tensor),
        P(tensor, dp),
        P(None, dp, tensor),
        P(tensor, dp),
        P(),
        P(dp, tensor),
        P(None, dp, tensor),
        P(tensor, dp),
        P(None, dp, tensor),
        P(tensor, dp),
        P(),
        P(dp, tensor),
        P(None, dp, tensor),
        P(tensor, dp),
        P(None, dp, tensor),
        P(tensor, dp),
    )
    out_specs = (
        P(dp, tensor, None),
        P(dp, tensor, None),
        P(),
        P(dp, tensor),
        P(None, dp, tensor),
        P(tensor, dp),
        P(None, dp, tensor),
        P(tensor, dp),
        P(),
        P(dp, tensor),
        P(None, dp, tensor),
        P(tensor, dp),
        P(None, dp, tensor),
        P(tensor, dp),
        P(),
        P(dp, tensor),
        P(None, dp, tensor),
        P(tensor, dp),
        P(None, dp, tensor),
        P(tensor, dp),
        P(),
        P(dp, tensor),
        P(None, dp, tensor),
        P(tensor, dp),
        P(None, dp, tensor),
        P(tensor, dp),
        P(),
        P(),
        P(),
    )
    return jax.shard_map(
        per_device, mesh=split, in_specs=in_specs, out_specs=out_specs, check_vma=False
    )
```
